256 devices in a mesh: row: 8 (over y, core), col: 32 (over x, z).
Axes of the slice: x: 4, y: 4, z: 8, core: 2. Of those that a mesh axis runs over, the one named last changes fastest.
Arguments:
- transmission: float32 [2, 2, 4096, 8192], P(None, None, 'row', 'col'), may hold values from -5 to 5
- probe_field: float32 [2, 256, 256], replicated, may hold values from -6 to 6
- prop_phase: float32 [256, 256], replicated, may hold values from -3.140625 to 3.140625
- amplitude: float32 [8, 32, 4, 256, 256], P('row', 'col'), may hold values from 0 to 2
- window_count: int32 [8, 32], P('row', 'col'), may hold values from 1 to 4
- offset_row: int32 [8, 32, 4], P('row', 'col'), may hold values from 0 to 384
- offset_col: int32 [8, 32, 4], P('row', 'col'), may hold values from 0 to 128
- window_batch: int32 [8, 32, 4], P('row', 'col'), may hold values from 0 to 2
Outputs:
- updated: float32 [2, 2, 4096, 8192], P(None, None, 'row', 'col')
The draws below stay inside these ranges and needn't reach their ends.
All inputs are finite; a program needn't handle non-finite values.
Results may differ from the reference program's by a relative error of at most 0.0003.
Values sent between devices are 32-bit elements; how exact they have to be, the bound alone decides.
No kernel may reach another device: no remote copies, remote signals or barrier semaphores. Data moves between devices by JAX's collectives and lax.ppermute only.
A program may use at most 64 MiB of HBM per device.

```python
import jax
import jax.numpy as jnp
from jax import lax

WIN = 256
STRIP = 128
TILE_R = 512
TILE_C = 256
SLOTS = 4
BATCHES = 3
TROWS = 8
TCOLS = 32
OBJ_R = 4096
OBJ_C = 8192
N_ROW = 8
N_COL = 32


def set_ends(drawn, key, smallest, top_value):
    dims = drawn.shape
    spot = [jax.random.randint(jax.random.fold_in(key, axis), (), 0, dims[axis]) for axis in range(len(dims))]
    drawn = drawn.at[tuple(spot)].set(smallest)
    longest = dims.index(max(dims))
    spot[longest] = (spot[longest] + 1) % dims[longest]
    return drawn.at[tuple(spot)].set(top_value)


def steps_of(own_key, extent, pieces, least, top_value):
    gain, own = 1.0, jax.random.fold_in(own_key, 6)
    for dim, blocks in pieces:
        heights = jnp.exp(jax.random.uniform(jax.random.fold_in(own, dim), (blocks,), jnp.float32, least / len(pieces), top_value / len(pieces)))
        gain = gain * jnp.repeat(heights, extent[dim] // blocks).reshape([-1 if axis == dim else 1 for axis in range(len(extent))])
    return gain


def bell_draw(own_key, dims, spread, most, cuts=(), kind=jnp.bfloat16):
    values = jax.random.normal(own_key, dims, jnp.float32) * spread
    if len(cuts) > 0:
        values = steps_of(own_key, dims, cuts, -0.22, 0.18) * values
    return jnp.clip(values, min=-most, max=most).astype(kind)


def setup_inputs(seed: int = 0) -> dict:
    streams_of = jax.random.split(jax.random.key(seed), 9)
    return {
        "transmission": bell_draw(streams_of[0], (2, 2, OBJ_R, OBJ_C), 0.7, 5.0, ((2, 8), (3, 32)), jnp.float32),
        "probe_field": bell_draw(streams_of[1], (2, WIN, WIN), 1.0, 6.0, (), jnp.float32),
        "prop_phase": jnp.clip(jax.random.uniform(streams_of[2], (WIN, WIN), jnp.float32, -3.140625, 3.140625), -3.140625, 3.140625),
        "amplitude": jnp.clip(2.0 * jax.random.uniform(streams_of[3], (TROWS, TCOLS, SLOTS, WIN, WIN), jnp.float32) ** steps_of(streams_of[3], (TROWS, TCOLS, SLOTS, WIN, WIN), ((0, 8), (1, 32)), -0.2, 0.2), 0.0, 2.0),
        "window_count": set_ends(jax.random.randint(streams_of[4], (TROWS, TCOLS), 1, SLOTS + 1), jax.random.fold_in(streams_of[4], 1), 1, SLOTS).astype(jnp.int32),
        "offset_row": set_ends(jax.random.randint(streams_of[5], (TROWS, TCOLS, SLOTS), 0, TILE_R - STRIP + 1), jax.random.fold_in(streams_of[5], 1), 0, TILE_R - STRIP).astype(jnp.int32),
        "offset_col": set_ends(jax.random.randint(streams_of[6], (TROWS, TCOLS, SLOTS), 0, TILE_C - STRIP + 1), jax.random.fold_in(streams_of[6], 1), 0, TILE_C - STRIP).astype(jnp.int32),
        "window_batch": set_ends(jax.random.randint(streams_of[7], (TROWS, TCOLS, SLOTS), 0, BATCHES), jax.random.fold_in(streams_of[7], 1), 0, BATCHES - 1).astype(jnp.int32),
    }


step_rate = 0.5


def forward_two(field):
    return jnp.fft.fft2(field, norm="ortho")


def inverse_two(field):
    return jnp.fft.ifft2(field, norm="ortho")


def window_terms(piece_one, piece_two, probe_c, propagator, measured):
    psi_one = probe_c * piece_one
    between = inverse_two(propagator * forward_two(psi_one))
    far = forward_two(between * piece_two)
    magnitude = jnp.abs(far)
    chi = far * (1.0 - measured / jnp.maximum(magnitude, 1.0))
    back_two = inverse_two(chi)
    grad_two = jnp.conj(between) * back_two
    back_mid = jnp.conj(piece_two) * back_two
    back_one = inverse_two(jnp.conj(propagator) * forward_two(back_mid))
    grad_one = jnp.conj(probe_c) * back_one
    return grad_one, grad_two


def reference(transmission, probe_field, prop_phase, amplitude, window_count, offset_row, offset_col, window_batch):
    slice_one = transmission[0, 0] + 1j * transmission[0, 1]
    slice_two = transmission[1, 0] + 1j * transmission[1, 1]
    probe_c = probe_field[0] + 1j * probe_field[1]
    propagator = jnp.cos(prop_phase) + 1j * jnp.sin(prop_phase)
    tile_rows = (jnp.arange(N_ROW, dtype=jnp.int32) * TILE_R)[:, None, None]
    tile_cols = (jnp.arange(N_COL, dtype=jnp.int32) * TILE_C)[None, :, None]
    glob_row = (tile_rows + offset_row).reshape(-1).astype(jnp.int32)
    glob_col = (tile_cols + offset_col).reshape(-1).astype(jnp.int32)
    slot_ids = jnp.arange(SLOTS, dtype=jnp.int32)[None, None, :]
    in_use = (slot_ids < window_count[:, :, None]).reshape(-1)
    batches = window_batch.reshape(-1)
    measured_all = amplitude.reshape(-1, WIN, WIN)
    for batch in range(BATCHES):
        padded_one = jnp.pad(slice_one, ((0, STRIP), (0, STRIP)))
        padded_two = jnp.pad(slice_two, ((0, STRIP), (0, STRIP)))
        weights = jnp.where(in_use & (batches == batch), 1.0, 0.0).astype(jnp.float32)

        def visit(carry, item):
            accum_one, accum_two = carry
            row_at, col_at, weight, measured = item
            piece_one = lax.dynamic_slice(padded_one, (row_at, col_at), (WIN, WIN))
            piece_two = lax.dynamic_slice(padded_two, (row_at, col_at), (WIN, WIN))
            grad_one, grad_two = window_terms(piece_one, piece_two, probe_c, propagator, measured)
            old_one = lax.dynamic_slice(accum_one, (row_at, col_at), (WIN, WIN))
            old_two = lax.dynamic_slice(accum_two, (row_at, col_at), (WIN, WIN))
            accum_one = lax.dynamic_update_slice(accum_one, old_one + weight * grad_one, (row_at, col_at))
            accum_two = lax.dynamic_update_slice(accum_two, old_two + weight * grad_two, (row_at, col_at))
            return (accum_one, accum_two), None

        start = (jnp.zeros_like(padded_one), jnp.zeros_like(padded_two))
        (accum_one, accum_two), _ = lax.scan(visit, start, (glob_row, glob_col, weights, measured_all))
        slice_one = slice_one - step_rate * accum_one[:OBJ_R, :OBJ_C]
        slice_two = slice_two - step_rate * accum_two[:OBJ_R, :OBJ_C]
    result = jnp.stack([jnp.stack([jnp.real(slice_one), jnp.imag(slice_one)]),
                        jnp.stack([jnp.real(slice_two), jnp.imag(slice_two)])])
    return result.astype(jnp.float32)
```

```python
import math

import jax
import jax.numpy as jnp
import numpy as np
from jax import lax
from jax.experimental import pallas as pl
from jax.experimental.pallas import tpu as pltpu
from jax.sharding import PartitionSpec as P

BATCHES = 3
WIN = 256
HALF = 128
SLOTS = 4
ROWS = 512
COLS = 256
EXT_R = 640
EXT_C = 384


cc = jnp.concatenate
f32 = jnp.float32
bf16 = jnp.bfloat16


def dft_tables():
    n = np.arange(HALF)
    even = np.exp(-2j * np.pi * (np.outer(n, n) % HALF) / HALF) / math.sqrt(WIN)
    odd = np.exp(-2j * np.pi * n / WIN)[:, None] * even
    out = []
    for m in (even, odd):
        full = np.block([[m.real, m.imag], [-m.imag, m.real]]).astype(np.float32)
        for t in (full, full.T):
            hi = t.astype(bf16)
            lo = (t - hi.astype(np.float32)).astype(bf16)
            out.append(np.stack([hi, lo]))
    return np.stack(out).reshape(2, 2, 2, WIN, WIN)


def order_matrix():
    source = np.concatenate([np.arange(0, WIN, 2), np.arange(1, WIN, 2)])
    m = np.zeros((WIN, WIN), np.float32)
    m[source, np.arange(WIN)] = 1.0
    return np.stack([m, m.T]).astype(bf16)


def halves(x):
    hi = x.astype(bf16)
    lo = (x - hi.astype(f32)).astype(bf16)
    return hi, lo


def dot_r(x, tab, which, trans):
    hi, lo = halves(x)
    th = tab[which, trans, 0]
    t = cc([th, th, tab[which, trans, 1]], 0)
    return jnp.dot(cc([hi, lo, hi], 1), t, preferred_element_type=f32)


def dot_l(tab, which, trans, x):
    hi, lo = halves(x)
    th = tab[which, trans, 0]
    t = cc([th, th, tab[which, trans, 1]], 1)
    return jnp.dot(t, cc([hi, lo, hi], 0), preferred_element_type=f32)


def forward_two(z, tab):
    re, im = z
    h = HALF
    a = dot_r(cc([re[:, :h] + re[:, h:], im[:, :h] + im[:, h:]], 1), tab, 0, 0)
    b = dot_r(cc([re[:, :h] - re[:, h:], im[:, :h] - im[:, h:]], 1), tab, 1, 0)
    re, im = cc([a[:, :h], b[:, :h]], 1), cc([a[:, h:], b[:, h:]], 1)
    a = dot_l(tab, 0, 1, cc([re[:h] + re[h:], im[:h] + im[h:]], 0))
    b = dot_l(tab, 1, 1, cc([re[:h] - re[h:], im[:h] - im[h:]], 0))
    return cc([a[:h], b[:h]], 0), cc([a[h:], b[h:]], 0)


def inverse_two(z, tab):
    re, im = z
    h = HALF
    a = dot_l(tab, 0, 0, cc([re[:h], im[:h]], 0))
    b = dot_l(tab, 1, 0, cc([re[h:], im[h:]], 0))
    s, d = a + b, a - b
    re, im = cc([s[:h], d[:h]], 0), cc([s[h:], d[h:]], 0)
    a = dot_r(cc([re[:, :h], im[:, :h]], 1), tab, 0, 1)
    b = dot_r(cc([re[:, h:], im[:, h:]], 1), tab, 1, 1)
    s, d = a + b, a - b
    return cc([s[:, :h], d[:, :h]], 1), cc([s[:, h:], d[:, h:]], 1)


def cmul(a, b):
    return a[0] * b[0] - a[1] * b[1], a[0] * b[1] + a[1] * b[0]


def cjmul(a, b):
    return a[0] * b[0] + a[1] * b[1], a[0] * b[1] - a[1] * b[0]


def place(r):
    base = pl.multiple_of(jnp.minimum(r // 8 * 8, EXT_R - WIN - 8), 8)
    return base, r - base


def load_window(ref, r, c):
    base, shift = place(r)
    out = []
    for p in range(2):
        t = ref[p, pl.ds(base, WIN + 8), :]
        t = pltpu.roll(t, lax.rem(EXT_C - c, EXT_C), 1)[:, :WIN]
        out.append(pltpu.roll(t, lax.rem(WIN + 8 - shift, WIN + 8), 0)[:WIN])
    return out


def add_window(ref, r, c, g):
    base, shift = place(r)
    for p in range(2):
        t = pltpu.roll(cc([g[p], jnp.zeros((8, WIN), f32)], 0), shift, 0)
        t = pltpu.roll(cc([t, jnp.zeros((WIN + 8, EXT_C - WIN), f32)], 1), c, 1)
        ref[p, pl.ds(base, WIN + 8), :] = ref[p, pl.ds(base, WIN + 8), :] + t


def each_window(batch, count, orow, ocol, wbatch, work):
    def step(s, _):
        @pl.when((s < count[0, 0]) & (wbatch[0, 0, s] == batch))
        def _():
            work(s, orow[0, 0, s], ocol[0, 0, s])

        return 0

    lax.fori_loop(0, SLOTS, step, 0)


def reorder(x, order):
    a = x.astype(bf16)
    rest = x - a.astype(f32)
    b = rest.astype(bf16)
    c = (rest - b.astype(f32)).astype(bf16)
    m = order[0]
    y = jnp.dot(a, m, preferred_element_type=f32)
    y = y + jnp.dot(b, m, preferred_element_type=f32)
    y = y + jnp.dot(c, m, preferred_element_type=f32)
    a = y.astype(bf16)
    rest = y - a.astype(f32)
    b = rest.astype(bf16)
    c = (rest - b.astype(f32)).astype(bf16)
    m = order[1]
    y = jnp.dot(m, a, preferred_element_type=f32)
    y = y + jnp.dot(m, b, preferred_element_type=f32)
    return y + jnp.dot(m, c, preferred_element_type=f32)


def prep_kernel(amp, phase, order, amp_out, prop_out):
    def step(s, _):
        amp_out[s] = reorder(amp[0, 0, s], order)
        return 0

    lax.fori_loop(0, SLOTS, step, 0)
    ph = reorder(phase[...], order)
    prop_out[0] = jnp.cos(ph)
    prop_out[1] = jnp.sin(ph)


def assemble(state, main, right, bottom):
    state[:, :ROWS, :COLS] = main[0]
    state[:, :ROWS, COLS:] = right[...]
    state[:, ROWS:, :] = bottom[...]


def update(state, old, grad, above, below, left, right):
    inside_r = jnp.where(lax.axis_index("row") < lax.axis_size("row") - 1, 0.5, 0.0).astype(f32)
    inside_c = jnp.where(lax.axis_index("col") < lax.axis_size("col") - 1, 0.5, 0.0).astype(f32)
    h = HALF
    for p in range(2):
        for top in range(0, EXT_R, h):
            rows = pl.ds(top, h)
            g = grad[p, rows, :]
            if top == 0:
                g = g + above[p]
            if top == ROWS:
                g = g + below[p]
            scale = inside_r if top == ROWS else jnp.float32(0.5)
            edge = inside_c * (scale * 2.0)
            state[p, rows, :h] = old[p, rows, :h] - scale * (g[:, :h] + left[p, rows, :])
            state[p, rows, h:COLS] = old[p, rows, h:COLS] - scale * g[:, h:COLS]
            state[p, rows, COLS:] = old[p, rows, COLS:] - edge * (g[:, COLS:] + right[p, rows, :])


def first_kernel(batch, first):
    def run(count, orow, ocol, wbatch, tab, probe, prop, *rest):
        between, state = rest[-2:]
        if first:
            assemble(state, *rest[:-2])
        else:
            update(state, *rest[:-2])

        def work(s, r, c):
            psi = cmul((probe[0], probe[1]), load_window(state, r, c))
            f = forward_two(psi, tab)
            bt = inverse_two(cmul((prop[0], prop[1]), f), tab)
            between[s, 0] = bt[0]
            between[s, 1] = bt[1]

        each_window(batch, count, orow, ocol, wbatch, work)

    return run


def second_kernel(batch, first):
    def run(count, orow, ocol, wbatch, tab, amp, between, *rest):
        grad, left, right, mid, state = rest[-5:]
        if first:
            assemble(state, *rest[:-5])
        else:
            update(state, *rest[:-5])
        grad[...] = jnp.zeros_like(grad)

        def work(s, r, c):
            w2 = load_window(state, r, c)
            bt = (between[s, 0], between[s, 1])
            far = forward_two(cmul(bt, w2), tab)
            power = far[0] * far[0] + far[1] * far[1]
            factor = 1.0 - amp[s] * lax.rsqrt(jnp.maximum(power, 1.0))
            back = inverse_two((far[0] * factor, far[1] * factor), tab)
            add_window(grad, r, c, cjmul((between[s, 0], between[s, 1]), back))
            m = cjmul(w2, back)
            mid[s, 0] = m[0]
            mid[s, 1] = m[1]

        each_window(batch, count, orow, ocol, wbatch, work)
        left[...] = grad[:, :, :HALF]
        right[...] = grad[:, :, COLS:]

    return run


def third_kernel(batch):
    def run(count, orow, ocol, wbatch, tab, probe, prop, mid, grad, top, bottom):
        grad[...] = jnp.zeros_like(grad)

        def work(s, r, c):
            f = forward_two((mid[s, 0], mid[s, 1]), tab)
            back = inverse_two(cjmul((prop[0], prop[1]), f), tab)
            add_window(grad, r, c, cjmul((probe[0], probe[1]), back))

        each_window(batch, count, orow, ocol, wbatch, work)
        top[...] = grad[:, :HALF, :]
        bottom[...] = grad[:, ROWS:, :]

    return run


def rows_of(grad, from_left, from_right, top, bottom):
    for out, at in ((top, 0), (bottom, ROWS)):
        rows = pl.ds(at, HALF)
        out[:, :, :HALF] = grad[:, rows, :HALF] + from_left[:, rows, :]
        out[:, :, HALF:COLS] = grad[:, rows, HALF:COLS]
        out[:, :, COLS:] = grad[:, rows, COLS:] + from_right[:, rows, :]


def cols_of(grad, from_above, from_below, left, right):
    for out, at in ((left, 0), (right, COLS)):
        cols = pl.ds(at, HALF)
        out[:, :HALF, :] = grad[:, :HALF, cols] + from_above[:, :, cols]
        out[:, HALF:ROWS, :] = grad[:, HALF:ROWS, cols]
        out[:, ROWS:, :] = grad[:, ROWS:, cols] + from_below[:, :, cols]


def last_kernel(state, grad, above, left, *rest):
    out = rest[-1]
    h = HALF
    for p in range(2):
        for top in range(0, ROWS, h):
            rows = pl.ds(top, h)
            g = grad[p, rows, :COLS]
            if top == 0:
                g = g + above[p, :, :COLS]
            out[0, p, rows, :h] = state[p, rows, :h] - 0.5 * (g[:, :h] + left[p, rows, :])
            out[0, p, rows, h:] = state[p, rows, h:COLS] - 0.5 * g[:, h:]


VM = pl.BlockSpec(memory_space=pltpu.VMEM)
SM = pl.BlockSpec(memory_space=pltpu.SMEM)
EXT = jax.ShapeDtypeStruct((2, EXT_R, EXT_C), f32)
SIDE = jax.ShapeDtypeStruct((2, EXT_R, HALF), f32)
FLAT = jax.ShapeDtypeStruct((2, HALF, EXT_C), f32)
PLANES = jax.ShapeDtypeStruct((SLOTS, 2, WIN, WIN), f32)
PARAMS = pltpu.CompilerParams(vmem_limit_bytes=60 * 2**20)


def call(kernel, name, scalars, arrays, outs):
    return pl.pallas_call(
        kernel,
        in_specs=[SM] * len(scalars) + [VM] * len(arrays),
        out_specs=[VM] * len(outs),
        out_shape=outs,
        compiler_params=PARAMS,
        name=name,
    )(*scalars, *arrays)


def from_behind(array, axis, by):
    size = lax.axis_size(axis)
    pairs = [(i, i + by) for i in range(size) if 0 <= i + by < size]
    return lax.ppermute(array, axis, pairs)


def body(transmission, probe, phase, amplitude, count, orow, ocol, wbatch):
    tab = jnp.asarray(dft_tables())
    order = jnp.asarray(order_matrix())
    scalars = (count, orow, ocol, wbatch)
    main = [transmission[0:1], transmission[1:2]]
    right = [from_behind(m[0, :, :, :HALF], "col", -1) for m in main]
    bottom = [
        from_behind(cc([m[0, :, :HALF, :], r[:, :HALF, :]], 2), "row", -1)
        for m, r in zip(main, right)
    ]
    amp, prop = call(
        prep_kernel,
        "prep",
        (),
        (amplitude, phase, order),
        [
            jax.ShapeDtypeStruct((SLOTS, WIN, WIN), f32),
            jax.ShapeDtypeStruct((2, WIN, WIN), f32),
        ],
    )
    parts1 = (main[0], right[0], bottom[0])
    parts2 = (main[1], right[1], bottom[1])
    for b in range(BATCHES):
        between, state1 = call(
            first_kernel(b, b == 0), f"first{b}", scalars, (tab, probe, prop, *parts1), [PLANES, EXT]
        )
        grad2, left2, right2, mid, state2 = call(
            second_kernel(b, b == 0),
            f"second{b}",
            scalars,
            (tab, amp, between, *parts2),
            [EXT, SIDE, SIDE, PLANES, EXT],
        )
        from_left2 = from_behind(right2, "col", 1)
        grad1, top1, bottom1 = call(
            third_kernel(b), f"third{b}", scalars, (tab, probe, prop, mid), [EXT, FLAT, FLAT]
        )
        from_above1 = from_behind(bottom1, "row", 1)
        if b == BATCHES - 1:
            break
        from_right2 = from_behind(left2, "col", -1)
        from_below1 = from_behind(top1, "row", -1)
        left1, right1 = call(cols_of, f"cols{b}", (), (grad1, from_above1, from_below1), [SIDE, SIDE])
        from_left1 = from_behind(right1, "col", 1)
        from_right1 = from_behind(left1, "col", -1)
        top2, bottom2 = call(rows_of, f"rows{b}", (), (grad2, from_left2, from_right2), [FLAT, FLAT])
        from_above2 = from_behind(bottom2, "row", 1)
        from_below2 = from_behind(top2, "row", -1)
        parts1 = (state1, grad1, from_above1, from_below1, from_left1, from_right1)
        parts2 = (state2, grad2, from_above2, from_below2, from_left2, from_right2)
    h = HALF
    send1 = cc([grad1[:, :h, COLS:] + from_above1[:, :, COLS:], grad1[:, h:ROWS, COLS:]], 1)
    from_left1 = from_behind(send1, "col", 1)
    send2 = cc([grad2[:, ROWS:, :h] + from_left2[:, ROWS:, :], grad2[:, ROWS:, h:COLS]], 2)
    from_above2 = from_behind(send2, "row", 1)
    out_shape = jax.ShapeDtypeStruct((2, 2, ROWS, COLS), f32)
    whole = [VM] * 4
    out = pl.pallas_call(
        last_kernel,
        grid=(1,),
        in_specs=whole,
        out_specs=pl.BlockSpec((1, 2, ROWS, COLS), lambda i: (1, 0, 0, 0)),
        out_shape=out_shape,
        compiler_params=PARAMS,
        name="last2",
    )(state2, grad2, from_above2, from_left2)
    return pl.pallas_call(
        last_kernel,
        grid=(1,),
        in_specs=whole + [pl.BlockSpec(memory_space=pl.ANY)],
        out_specs=pl.BlockSpec((1, 2, ROWS, COLS), lambda i: (0, 0, 0, 0)),
        out_shape=out_shape,
        input_output_aliases={4: 0},
        compiler_params=PARAMS,
        name="last1",
    )(state1, grad1, from_above1, from_left1, out)


def solution(mesh):
    in_specs = (
        P(None, None, "row", "col"),
        P(),
        P(),
        P("row", "col", None, None, None),
        P("row", "col"),
        P("row", "col", None),
        P("row", "col", None),
        P("row", "col", None),
    )
    out_specs = P(None, None, "row", "col")
    return jax.shard_map(body, mesh=mesh, in_specs=in_specs, out_specs=out_specs, check_vma=False)
```

```python
import math

import jax
import jax.numpy as jnp
import numpy as np
from jax import lax
from jax.experimental import pallas as pl
from jax.experimental.pallas import tpu as pltpu
from jax.sharding import PartitionSpec as P

BATCHES = 3
WIN = 256
HALF = 128
SLOTS = 4
ROWS = 512
COLS = 256
EXT_R = 640
EXT_C = 384


cc = jnp.concatenate
f32 = jnp.float32
bf16 = jnp.bfloat16


def dft_tables():
    n = np.arange(HALF)
    even = np.exp(-2j * np.pi * (np.outer(n, n) % HALF) / HALF) / math.sqrt(WIN)
    odd = np.exp(-2j * np.pi * n / WIN)[:, None] * even
    out = []
    for m in (even, odd):
        full = np.block([[m.real, m.imag], [-m.imag, m.real]]).astype(np.float32)
        for t in (full, full.T):
            hi = t.astype(bf16)
            lo = (t - hi.astype(np.float32)).astype(bf16)
            out.append(np.stack([hi, lo]))
    return np.stack(out).reshape(2, 2, 2, WIN, WIN)


def order_matrix():
    source = np.concatenate([np.arange(0, WIN, 2), np.arange(1, WIN, 2)])
    m = np.zeros((WIN, WIN), np.float32)
    m[source, np.arange(WIN)] = 1.0
    return np.stack([m, m.T]).astype(bf16)


def halves(x):
    hi = x.astype(bf16)
    lo = (x - hi.astype(f32)).astype(bf16)
    return hi, lo


def dot_r(x, tab, which, trans):
    hi, lo = halves(x)
    th = tab[which, trans, 0]
    t = cc([th, th, tab[which, trans, 1]], 0)
    return jnp.dot(cc([hi, lo, hi], 1), t, preferred_element_type=f32)


def dot_l(tab, which, trans, x):
    hi, lo = halves(x)
    th = tab[which, trans, 0]
    t = cc([th, th, tab[which, trans, 1]], 1)
    return jnp.dot(t, cc([hi, lo, hi], 0), preferred_element_type=f32)


def forward_two(z, tab):
    re, im = z
    h = HALF
    a = dot_r(cc([re[:, :h] + re[:, h:], im[:, :h] + im[:, h:]], 1), tab, 0, 0)
    b = dot_r(cc([re[:, :h] - re[:, h:], im[:, :h] - im[:, h:]], 1), tab, 1, 0)
    re, im = cc([a[:, :h], b[:, :h]], 1), cc([a[:, h:], b[:, h:]], 1)
    a = dot_l(tab, 0, 1, cc([re[:h] + re[h:], im[:h] + im[h:]], 0))
    b = dot_l(tab, 1, 1, cc([re[:h] - re[h:], im[:h] - im[h:]], 0))
    return cc([a[:h], b[:h]], 0), cc([a[h:], b[h:]], 0)


def inverse_two(z, tab):
    re, im = z
    h = HALF
    a = dot_l(tab, 0, 0, cc([re[:h], im[:h]], 0))
    b = dot_l(tab, 1, 0, cc([re[h:], im[h:]], 0))
    s, d = a + b, a - b
    re, im = cc([s[:h], d[:h]], 0), cc([s[h:], d[h:]], 0)
    a = dot_r(cc([re[:, :h], im[:, :h]], 1), tab, 0, 1)
    b = dot_r(cc([re[:, h:], im[:, h:]], 1), tab, 1, 1)
    s, d = a + b, a - b
    return cc([s[:, :h], d[:, :h]], 1), cc([s[:, h:], d[:, h:]], 1)


def cmul(a, b):
    return a[0] * b[0] - a[1] * b[1], a[0] * b[1] + a[1] * b[0]


def cjmul(a, b):
    return a[0] * b[0] + a[1] * b[1], a[0] * b[1] - a[1] * b[0]


def place(r):
    base = pl.multiple_of(jnp.minimum(r // 8 * 8, EXT_R - WIN - 8), 8)
    return base, r - base


def load_window(ref, first, r, c):
    base, shift = place(r)
    out = []
    for p in (first, first + 1):
        t = ref[p, pl.ds(base, WIN + 8), :]
        t = pltpu.roll(t, lax.rem(EXT_C - c, EXT_C), 1)[:, :WIN]
        out.append(pltpu.roll(t, lax.rem(WIN + 8 - shift, WIN + 8), 0)[:WIN])
    return out


def add_window(ref, first, r, c, g):
    base, shift = place(r)
    for p in (first, first + 1):
        t = pltpu.roll(cc([g[p - first], jnp.zeros((8, WIN), f32)], 0), shift, 0)
        t = pltpu.roll(cc([t, jnp.zeros((WIN + 8, EXT_C - WIN), f32)], 1), c, 1)
        ref[p, pl.ds(base, WIN + 8), :] = ref[p, pl.ds(base, WIN + 8), :] + t


def reorder(x, order):
    a = x.astype(bf16)
    rest = x - a.astype(f32)
    b = rest.astype(bf16)
    c = (rest - b.astype(f32)).astype(bf16)
    m = order[0]
    y = jnp.dot(a, m, preferred_element_type=f32)
    y = y + jnp.dot(b, m, preferred_element_type=f32)
    y = y + jnp.dot(c, m, preferred_element_type=f32)
    a = y.astype(bf16)
    rest = y - a.astype(f32)
    b = rest.astype(bf16)
    c = (rest - b.astype(f32)).astype(bf16)
    m = order[1]
    y = jnp.dot(m, a, preferred_element_type=f32)
    y = y + jnp.dot(m, b, preferred_element_type=f32)
    return y + jnp.dot(m, c, preferred_element_type=f32)


def prep_kernel(amp, phase, order, amp_out, prop_out):
    def step(s, _):
        amp_out[s] = reorder(amp[0, 0, s], order)
        return 0

    lax.fori_loop(0, SLOTS, step, 0)
    ph = reorder(phase[...], order)
    prop_out[0] = jnp.cos(ph)
    prop_out[1] = jnp.sin(ph)


def inside(axis):
    return lax.axis_index(axis) < lax.axis_size(axis) - 1


def assemble_kernel(main, right_top, right_rest, bottom, state):
    for p in range(4):
        q = (p // 2, p % 2)
        state[p, :ROWS, :COLS] = main[q]
        state[p, :HALF, COLS:] = right_top[p]
        state[p, HALF:ROWS, COLS:] = right_rest[p]
        state[p, ROWS:, :] = bottom[p]


def batch_kernel(batch, first):
    def run(count, orow, ocol, wbatch, tab, probe, prop, amp, *rest):
        if first:
            (old,) = rest[:1]
            state, grad, side_l, side_r, top, bottom = rest[1:]
            state = old
        else:
            old, mid_l, mid_r, end_l, end_r = rest[:5]
            state, grad, side_l, side_r, top, bottom = rest[5:]
            scale = jnp.where(inside("col"), 0.5, 0.0).astype(f32)
            drop = jnp.where(inside("row"), 1.0, 0.0).astype(f32)
            for p in range(4):
                for cols, fac, mid, end in (
                    (pl.ds(0, HALF), jnp.float32(0.5), mid_l, end_l),
                    (pl.ds(COLS, HALF), scale, mid_r, end_r),
                ):
                    state[p, :HALF, cols] = old[p, :HALF, cols] - fac * end[p, :HALF]
                    state[p, HALF:ROWS, cols] = old[p, HALF:ROWS, cols] - fac * mid[p]
                    state[p, ROWS:, cols] = old[p, ROWS:, cols] - (fac * drop) * end[p, HALF:]
        grad[...] = jnp.zeros_like(grad)

        def step(s, _):
            @pl.when((s < count[0, 0]) & (wbatch[0, 0, s] == batch))
            def _():
                r = orow[0, 0, s]
                c = ocol[0, 0, s]
                psi = cmul((probe[0], probe[1]), load_window(state, 0, r, c))
                f = forward_two(psi, tab)
                bt = inverse_two(cmul((prop[0], prop[1]), f), tab)
                w2 = load_window(state, 2, r, c)
                far = forward_two(cmul(bt, w2), tab)
                power = far[0] * far[0] + far[1] * far[1]
                factor = 1.0 - amp[s] * lax.rsqrt(jnp.maximum(power, 1.0))
                back = inverse_two((far[0] * factor, far[1] * factor), tab)
                add_window(grad, 2, r, c, cjmul(bt, back))
                f = forward_two(cjmul(w2, back), tab)
                back = inverse_two(cjmul((prop[0], prop[1]), f), tab)
                add_window(grad, 0, r, c, cjmul((probe[0], probe[1]), back))

            return 0

        lax.fori_loop(0, SLOTS, step, 0)
        side_l[...] = grad[:, HALF:ROWS, :HALF]
        side_r[...] = grad[:, HALF:ROWS, COLS:]
        top[...] = grad[:, :HALF, :]
        bottom[...] = grad[:, ROWS:, :]

    return run


def settle_kernel(state, grad, above, below, out, end_l, end_r):
    in_r = jnp.where(inside("row"), 0.5, 0.0).astype(f32)
    in_c = jnp.where(inside("col"), 1.0, 0.0).astype(f32)
    h = HALF
    for p in range(4):
        for at in range(0, EXT_R, h):
            rows = pl.ds(at, h)
            g = grad[p, rows, :]
            if at == 0:
                g = g + above[p]
                end_l[p, :h] = g[:, :h]
                end_r[p, :h] = g[:, COLS:]
            if at == ROWS:
                g = g + below[p]
                end_l[p, h:] = g[:, :h]
                end_r[p, h:] = g[:, COLS:]
            scale = in_r if at == ROWS else jnp.float32(0.5)
            out[p, rows, :COLS] = state[p, rows, :COLS] - scale * g[:, :COLS]
            out[p, rows, COLS:] = state[p, rows, COLS:] - (scale * in_c) * g[:, COLS:]


def final_settle_kernel(state, grad, above, out, end_r):
    h = HALF
    for p in range(4):
        for at in range(0, ROWS, h):
            rows = pl.ds(at, h)
            g = grad[p, rows, :]
            if at == 0:
                g = g + above[p]
                end_r[p] = g[:, COLS:]
            out[p, rows] = state[p, rows, :COLS] - 0.5 * g[:, :COLS]


def last_kernel(state, mid, end, out):
    h = HALF
    for p in range(4):
        q = (p // 2, p % 2)
        out[(*q, slice(0, h), slice(0, h))] = state[p, :h, :h] - 0.5 * end[p]
        out[(*q, slice(h, ROWS), slice(0, h))] = state[p, h:, :h] - 0.5 * mid[p]
        out[(*q, slice(0, ROWS), slice(h, COLS))] = state[p, :, h:]


VM = pl.BlockSpec(memory_space=pltpu.VMEM)
SM = pl.BlockSpec(memory_space=pltpu.SMEM)
EXT = (4, EXT_R, EXT_C)
FLAT = (4, HALF, EXT_C)
MIDS = (4, ROWS - HALF, HALF)
ENDS = (4, 2 * HALF, HALF)


def call(kernel, scalars, arrays, outs, alias=None, limit=24):
    return pl.pallas_call(
        kernel,
        in_specs=[SM] * len(scalars) + [VM] * len(arrays),
        out_specs=[VM] * len(outs),
        out_shape=[jax.ShapeDtypeStruct(s, f32) for s in outs],
        input_output_aliases=alias or {},
        compiler_params=pltpu.CompilerParams(vmem_limit_bytes=limit * 2**20),
    )(*scalars, *arrays)


def from_behind(array, axis, by):
    size = lax.axis_size(axis)
    pairs = [(i, i + by) for i in range(size) if 0 <= i + by < size]
    return lax.ppermute(array, axis, pairs)


def body(transmission, probe, phase, amplitude, count, orow, ocol, wbatch):
    tab = jnp.asarray(dft_tables())
    order = jnp.asarray(order_matrix())
    scalars = (count, orow, ocol, wbatch)
    h = HALF
    planes = transmission.reshape(4, ROWS, COLS)
    right_top = from_behind(planes[:, :h, :h], "col", -1)
    right_rest = from_behind(planes[:, h:, :h], "col", -1)
    amp, prop = call(
        prep_kernel, (), (amplitude, phase, order), [(SLOTS, WIN, WIN), (2, WIN, WIN)]
    )
    low = cc([planes[:, :h, :], right_top], 2)
    bottom = from_behind(low, "row", -1)
    (state,) = call(
        assemble_kernel, (), (transmission, right_top, right_rest, bottom), [EXT]
    )
    parts = ()
    for b in range(BATCHES):
        state, grad, side_l, side_r, top, low = call(
            batch_kernel(b, b == 0),
            scalars,
            (tab, probe, prop, amp, state, *parts),
            [EXT, EXT, MIDS, MIDS, FLAT, FLAT],
            {8: 0},
        )
        mid_l = from_behind(side_r, "col", 1)
        above = from_behind(low, "row", 1)
        if b == BATCHES - 1:
            break
        mid_r = from_behind(side_l, "col", -1)
        below = from_behind(top, "row", -1)
        state, end_l, end_r = call(
            settle_kernel, (), (state, grad, above, below), [EXT, ENDS, ENDS], {0: 0}
        )
        parts = (
            mid_l, mid_r, from_behind(end_r, "col", 1), from_behind(end_l, "col", -1)
        )
    main, end_r = call(
        final_settle_kernel, (), (state, grad, above), [(4, ROWS, COLS), (4, h, h)]
    )
    end_l = from_behind(end_r, "col", 1)
    return call(last_kernel, (), (main, mid_l, end_l), [(2, 2, ROWS, COLS)])[0]


def solution(mesh):
    in_specs = (
        P(None, None, "row", "col"),
        P(),
        P(),
        P("row", "col", None, None, None),
        P("row", "col"),
        P("row", "col", None),
        P("row", "col", None),
        P("row", "col", None),
    )
    out_specs = P(None, None, "row", "col")
    return jax.shard_map(body, mesh=mesh, in_specs=in_specs, out_specs=out_specs, check_vma=False)
```

```python
import math

import jax
import jax.numpy as jnp
import numpy as np
from jax import lax
from jax.experimental import pallas as pl
from jax.experimental.pallas import tpu as pltpu
from jax.sharding import PartitionSpec as P

BATCHES = 3
WIN = 256
HALF = 128
SLOTS = 4
ROWS = 512
COLS = 256
EXT_R = 640
EXT_C = 384


cc = jnp.concatenate
f32 = jnp.float32
bf16 = jnp.bfloat16


def dft_tables():
    n = np.arange(HALF)
    even = np.exp(-2j * np.pi * (np.outer(n, n) % HALF) / HALF) / math.sqrt(WIN)
    odd = np.exp(-2j * np.pi * n / WIN)[:, None] * even
    out = []
    for m in (even, odd):
        full = np.block([[m.real, m.imag], [-m.imag, m.real]]).astype(np.float32)
        for t in (full, full.T):
            hi = t.astype(bf16)
            lo = (t - hi.astype(np.float32)).astype(bf16)
            out.append(np.stack([hi, lo]))
    return np.stack(out).reshape(2, 2, 2, WIN, WIN)


def order_matrix():
    source = np.concatenate([np.arange(0, WIN, 2), np.arange(1, WIN, 2)])
    m = np.zeros((WIN, WIN), np.float32)
    m[source, np.arange(WIN)] = 1.0
    return np.stack([m, m.T]).astype(bf16)


def halves(x):
    hi = x.astype(bf16)
    lo = (x - hi.astype(f32)).astype(bf16)
    return hi, lo


def dot_r(x, tab, which, trans):
    hi, lo = halves(x)
    th = tab[which, trans, 0]
    t = cc([th, th, tab[which, trans, 1]], 0)
    return jnp.dot(cc([hi, lo, hi], 1), t, preferred_element_type=f32)


def dot_l(tab, which, trans, x):
    hi, lo = halves(x)
    th = tab[which, trans, 0]
    t = cc([th, th, tab[which, trans, 1]], 1)
    return jnp.dot(t, cc([hi, lo, hi], 0), preferred_element_type=f32)


def forward_two(z, tab):
    re, im = z
    h = HALF
    a = dot_r(cc([re[:, :h] + re[:, h:], im[:, :h] + im[:, h:]], 1), tab, 0, 0)
    b = dot_r(cc([re[:, :h] - re[:, h:], im[:, :h] - im[:, h:]], 1), tab, 1, 0)
    re, im = cc([a[:, :h], b[:, :h]], 1), cc([a[:, h:], b[:, h:]], 1)
    a = dot_l(tab, 0, 1, cc([re[:h] + re[h:], im[:h] + im[h:]], 0))
    b = dot_l(tab, 1, 1, cc([re[:h] - re[h:], im[:h] - im[h:]], 0))
    return cc([a[:h], b[:h]], 0), cc([a[h:], b[h:]], 0)


def inverse_two(z, tab):
    re, im = z
    h = HALF
    a = dot_l(tab, 0, 0, cc([re[:h], im[:h]], 0))
    b = dot_l(tab, 1, 0, cc([re[h:], im[h:]], 0))
    s, d = a + b, a - b
    re, im = cc([s[:h], d[:h]], 0), cc([s[h:], d[h:]], 0)
    a = dot_r(cc([re[:, :h], im[:, :h]], 1), tab, 0, 1)
    b = dot_r(cc([re[:, h:], im[:, h:]], 1), tab, 1, 1)
    s, d = a + b, a - b
    return cc([s[:, :h], d[:, :h]], 1), cc([s[:, h:], d[:, h:]], 1)


def cmul(a, b):
    return a[0] * b[0] - a[1] * b[1], a[0] * b[1] + a[1] * b[0]


def cjmul(a, b):
    return a[0] * b[0] + a[1] * b[1], a[0] * b[1] - a[1] * b[0]


def place(r):
    base = pl.multiple_of(jnp.minimum(r // 8 * 8, EXT_R - WIN - 8), 8)
    return base, r - base


def lanes_left(x, c):
    keep = lax.broadcasted_iota(jnp.int32, (x.shape[0], HALF), 1) < HALF - c
    turn = lax.rem(HALF - c, HALF)
    a, b, d = [pltpu.roll(x[:, i * HALF : (i + 1) * HALF], turn, 1) for i in range(3)]
    return cc([jnp.where(keep, a, b), jnp.where(keep, b, d)], 1)


def lanes_right(x, c):
    keep = lax.broadcasted_iota(jnp.int32, (x.shape[0], HALF), 1) >= c
    turn = lax.rem(c, HALF)
    a, b = [pltpu.roll(x[:, i * HALF : (i + 1) * HALF], turn, 1) for i in range(2)]
    none = jnp.zeros_like(a)
    return cc([jnp.where(keep, a, none), jnp.where(keep, b, a), jnp.where(keep, none, b)], 1)


def rows_up(x, shift):
    y = x.reshape(WIN // 8 + 1, 8, x.shape[1])
    y = pltpu.roll(y, lax.rem(8 - shift, 8), 1)
    keep = lax.broadcasted_iota(jnp.int32, (WIN // 8, 8, x.shape[1]), 1) < 8 - shift
    return jnp.where(keep, y[:-1], y[1:]).reshape(WIN, x.shape[1])


def rows_down(x, shift):
    y = x.reshape(WIN // 8, 8, x.shape[1])
    y = pltpu.roll(y, lax.rem(shift, 8), 1)
    none = jnp.zeros((1, 8, x.shape[1]), f32)
    keep = lax.broadcasted_iota(jnp.int32, (WIN // 8 + 1, 8, x.shape[1]), 1) >= shift
    return jnp.where(keep, cc([y, none], 0), cc([none, y], 0)).reshape(WIN + 8, x.shape[1])


def load_window(ref, first, r, c):
    base, shift = place(r)
    out = []
    for p in (first, first + 1):
        t = lanes_left(ref[p, pl.ds(base, WIN + 8), :], c)
        out.append(rows_up(t, shift))
    return out


def add_window(ref, first, r, c, g):
    base, shift = place(r)
    for p in (first, first + 1):
        t = lanes_right(rows_down(g[p - first], shift), c)
        ref[p, pl.ds(base, WIN + 8), :] = ref[p, pl.ds(base, WIN + 8), :] + t


def reorder(x, order):
    a = x.astype(bf16)
    rest = x - a.astype(f32)
    b = rest.astype(bf16)
    c = (rest - b.astype(f32)).astype(bf16)
    m = order[0]
    y = jnp.dot(a, m, preferred_element_type=f32)
    y = y + jnp.dot(b, m, preferred_element_type=f32)
    y = y + jnp.dot(c, m, preferred_element_type=f32)
    a = y.astype(bf16)
    rest = y - a.astype(f32)
    b = rest.astype(bf16)
    c = (rest - b.astype(f32)).astype(bf16)
    m = order[1]
    y = jnp.dot(m, a, preferred_element_type=f32)
    y = y + jnp.dot(m, b, preferred_element_type=f32)
    return y + jnp.dot(m, c, preferred_element_type=f32)


def prep_kernel(amp, phase, order, amp_out, prop_out):
    def step(s, _):
        amp_out[s] = reorder(amp[0, 0, s], order)
        return 0

    lax.fori_loop(0, SLOTS, step, 0)
    ph = reorder(phase[...], order)
    prop_out[0] = jnp.cos(ph)
    prop_out[1] = jnp.sin(ph)


def inside(axis):
    return lax.axis_index(axis) < lax.axis_size(axis) - 1


def assemble_kernel(main, right_top, right_rest, bottom, state):
    for p in range(4):
        q = (p // 2, p % 2)
        state[p, :ROWS, :COLS] = main[q]
        state[p, :HALF, COLS:] = right_top[p]
        state[p, HALF:ROWS, COLS:] = right_rest[p]
        state[p, ROWS:, :] = bottom[p]


def batch_kernel(batch, first, final):
    def run(count, orow, ocol, wbatch, tab, probe, prop, amp, *rest):
        if first:
            state, grad, side_l, side_r, *edges = rest[1:]
        else:
            old, mid_l, mid_r, end_l, end_r, core_a, core_b = rest[:7]
            outs = rest[7:]
            state, grad, side_l, side_r, *edges = (*outs[:2], None, *outs[2:]) if final else outs
            scale = jnp.where(inside("col"), 0.5, 0.0).astype(f32)
            drop = jnp.where(inside("row"), 1.0, 0.0).astype(f32)
            for p in range(4):
                for cols, fac, mid, end in (
                    (pl.ds(0, HALF), jnp.float32(0.5), mid_l, end_l),
                    (pl.ds(COLS, HALF), scale, mid_r, end_r),
                ):
                    state[p, :HALF, cols] = old[p, :HALF, cols] - fac * end[p, :HALF]
                    state[p, HALF:ROWS, cols] = old[p, HALF:ROWS, cols] - fac * mid[p]
                    state[p, ROWS:, cols] = old[p, ROWS:, cols] - (fac * drop) * end[p, HALF:]
                cols = pl.ds(HALF, HALF)
                state[p, :HALF, cols] = old[p, :HALF, cols] - 0.5 * core_a[p]
                state[p, ROWS:, cols] = old[p, ROWS:, cols] - (0.5 * drop) * core_b[p]
        grad[...] = jnp.zeros_like(grad)

        def step(s, _):
            @pl.when((s < count[0, 0]) & (wbatch[0, 0, s] == batch))
            def _():
                r = orow[0, 0, s]
                c = ocol[0, 0, s]
                psi = cmul((probe[0], probe[1]), load_window(state, 0, r, c))
                f = forward_two(psi, tab)
                bt = inverse_two(cmul((prop[0], prop[1]), f), tab)
                w2 = load_window(state, 2, r, c)
                far = forward_two(cmul(bt, w2), tab)
                power = far[0] * far[0] + far[1] * far[1]
                factor = 1.0 - amp[s] * lax.rsqrt(jnp.maximum(power, 1.0))
                back = inverse_two((far[0] * factor, far[1] * factor), tab)
                add_window(grad, 2, r, c, cjmul(bt, back))
                f = forward_two(cjmul(w2, back), tab)
                back = inverse_two(cjmul((prop[0], prop[1]), f), tab)
                add_window(grad, 0, r, c, cjmul((probe[0], probe[1]), back))

            return 0

        lax.fori_loop(0, SLOTS, step, 0)
        side_r[...] = grad[:, HALF:ROWS, COLS:]
        if final:
            corner, low = edges
            corner[...] = grad[:, ROWS:, COLS:]
            low[...] = grad[:, ROWS:, :COLS]
        else:
            side_l[...] = grad[:, HALF:ROWS, :HALF]
            top, bottom, top_core, bottom_core = edges
            for out, core, rows in ((top, top_core, pl.ds(0, HALF)), (bottom, bottom_core, pl.ds(ROWS, HALF))):
                out[:, :, :HALF] = grad[:, rows, :HALF]
                out[:, :, HALF:] = grad[:, rows, COLS:]
                core[...] = grad[:, rows, HALF:COLS]

    return run


def settle_kernel(state, grad, above, below, out, end_l, end_r):
    in_r = jnp.where(inside("row"), 0.5, 0.0).astype(f32)
    in_c = jnp.where(inside("col"), 1.0, 0.0).astype(f32)
    h = HALF
    for p in range(4):
        for at, near, ends in ((0, above, pl.ds(0, h)), (h, None, None), (ROWS, below, pl.ds(h, h))):
            rows = pl.ds(at, ROWS - h if near is None else h)
            left, mid, right = grad[p, rows, :h], grad[p, rows, h:COLS], grad[p, rows, COLS:]
            if near is not None:
                left = left + near[p, :, :h]
                right = right + near[p, :, h:]
                end_l[p, ends] = left
                end_r[p, ends] = right
            scale = in_r if at == ROWS else jnp.float32(0.5)
            out[p, rows, :h] = state[p, rows, :h] - scale * left
            out[p, rows, h:COLS] = state[p, rows, h:COLS] - scale * mid
            out[p, rows, COLS:] = state[p, rows, COLS:] - (scale * in_c) * right


def final_settle_kernel(state, grad, corner, out, end_r):
    for p in range(4):
        end_r[p] = grad[p, :HALF, COLS:] + corner[p]
        out[p] = state[p, :ROWS, :COLS] - 0.5 * grad[p, :ROWS, :COLS]


def last_kernel(state, mid, end, low, out):
    h = HALF
    for p in range(4):
        q = (p // 2, p % 2)
        out[(*q, slice(0, h), slice(0, h))] = state[p, :h, :h] - 0.5 * (end[p] + low[p, :, :h])
        out[(*q, slice(h, ROWS), slice(0, h))] = state[p, h:, :h] - 0.5 * mid[p]
        out[(*q, slice(0, h), slice(h, COLS))] = state[p, :h, h:] - 0.5 * low[p, :, h:]
        out[(*q, slice(h, ROWS), slice(h, COLS))] = state[p, h:, h:]


VM = pl.BlockSpec(memory_space=pltpu.VMEM)
SM = pl.BlockSpec(memory_space=pltpu.SMEM)
EXT = (4, EXT_R, EXT_C)
EDGE = (4, HALF, 2 * HALF)
CORE = (4, HALF, HALF)
MIDS = (4, ROWS - HALF, HALF)
ENDS = (4, 2 * HALF, HALF)


def call(kernel, scalars, arrays, outs, alias=None, limit=24):
    return pl.pallas_call(
        kernel,
        in_specs=[SM] * len(scalars) + [VM] * len(arrays),
        out_specs=[VM] * len(outs),
        out_shape=[jax.ShapeDtypeStruct(s, f32) for s in outs],
        input_output_aliases=alias or {},
        compiler_params=pltpu.CompilerParams(vmem_limit_bytes=limit * 2**20),
    )(*scalars, *arrays)


def from_behind(array, axis, by):
    size = lax.axis_size(axis)
    pairs = [(i, i + by) for i in range(size) if 0 <= i + by < size]
    return lax.ppermute(array, axis, pairs)


def body(transmission, probe, phase, amplitude, count, orow, ocol, wbatch):
    tab = jnp.asarray(dft_tables())
    order = jnp.asarray(order_matrix())
    scalars = (count, orow, ocol, wbatch)
    h = HALF
    planes = transmission.reshape(4, ROWS, COLS)
    right_top = from_behind(planes[:, :h, :h], "col", -1)
    right_rest = from_behind(planes[:, h:, :h], "col", -1)
    amp, prop = call(prep_kernel, (), (amplitude, phase, order), [(SLOTS, WIN, WIN), (2, WIN, WIN)])
    low = cc([planes[:, :h, :], right_top], 2)
    bottom = from_behind(low, "row", -1)
    (state,) = call(assemble_kernel, (), (transmission, right_top, right_rest, bottom), [EXT])
    parts = ()
    for b in range(BATCHES):
        final = b == BATCHES - 1
        outs = [MIDS, CORE, EDGE] if final else [MIDS, MIDS, EDGE, EDGE, CORE, CORE]
        state, grad, *sent = call(
            batch_kernel(b, b == 0, final),
            scalars,
            (tab, probe, prop, amp, state, *parts),
            [EXT, EXT, *outs],
            {8: 0},
        )
        if final:
            side_r, corner, low = sent
            mid_l = from_behind(side_r, "col", 1)
            corner = from_behind(corner, "row", 1)
            main, end_r = call(
                final_settle_kernel, (), (state, grad, corner), [(4, ROWS, COLS), CORE]
            )
            end_l = from_behind(end_r, "col", 1)
            low = from_behind(low, "row", 1)
            break
        side_l, side_r, top, bottom, top_core, bottom_core = sent
        mid_l = from_behind(side_r, "col", 1)
        mid_r = from_behind(side_l, "col", -1)
        above = from_behind(bottom, "row", 1)
        below = from_behind(top, "row", -1)
        state, end_l, end_r = call(
            settle_kernel, (), (state, grad, above, below), [EXT, ENDS, ENDS], {0: 0}
        )
        parts = (
            mid_l,
            mid_r,
            from_behind(end_r, "col", 1),
            from_behind(end_l, "col", -1),
            from_behind(bottom_core, "row", 1),
            from_behind(top_core, "row", -1),
        )
    return call(last_kernel, (), (main, mid_l, end_l, low), [(2, 2, ROWS, COLS)])[0]


def solution(mesh):
    in_specs = (
        P(None, None, "row", "col"),
        P(),
        P(),
        P("row", "col", None, None, None),
        P("row", "col"),
        P("row", "col", None),
        P("row", "col", None),
        P("row", "col", None),
    )
    out_specs = P(None, None, "row", "col")
    return jax.shard_map(body, mesh=mesh, in_specs=in_specs, out_specs=out_specs, check_vma=False)
```

```python
import math

import jax
import jax.numpy as jnp
import numpy as np
from jax import lax
from jax.experimental import pallas as pl
from jax.experimental.pallas import tpu as pltpu
from jax.sharding import PartitionSpec as P

BATCHES = 3
WIN = 256
HALF = 128
SLOTS = 4
ROWS = 512
COLS = 256
EXT_R = 640
EXT_C = 384


cc = jnp.concatenate
f32 = jnp.float32
bf16 = jnp.bfloat16


def dft_tables():
    n = np.arange(HALF)
    even = np.exp(-2j * np.pi * (np.outer(n, n) % HALF) / HALF) / math.sqrt(WIN)
    odd = np.exp(-2j * np.pi * n / WIN)[:, None] * even
    out = []
    for m in (even, odd):
        full = np.block([[m.real, m.imag], [-m.imag, m.real]]).astype(np.float32)
        for t in (full, full.T):
            hi = t.astype(bf16)
            lo = (t - hi.astype(np.float32)).astype(bf16)
            out.append(np.stack([hi, lo]))
    return np.stack(out).reshape(2, 2, 2, WIN, WIN)


def order_matrix():
    source = np.concatenate([np.arange(0, WIN, 2), np.arange(1, WIN, 2)])
    m = np.zeros((WIN, WIN), np.float32)
    m[source, np.arange(WIN)] = 1.0
    return np.stack([m, m.T]).astype(bf16)


def halves(x):
    hi = x.astype(bf16)
    lo = (x - hi.astype(f32)).astype(bf16)
    return hi, lo


def dot_r(x, tab, which, trans):
    hi, lo = halves(x)
    th = tab[which, trans, 0]
    t = cc([th, th, tab[which, trans, 1]], 0)
    return jnp.dot(cc([hi, lo, hi], 1), t, preferred_element_type=f32)


def dot_l(tab, which, trans, x):
    hi, lo = halves(x)
    th = tab[which, trans, 0]
    t = cc([th, th, tab[which, trans, 1]], 1)
    return jnp.dot(t, cc([hi, lo, hi], 0), preferred_element_type=f32)


def forward_two(z, tab):
    re, im = z
    h = HALF
    a = dot_r(cc([re[:, :h] + re[:, h:], im[:, :h] + im[:, h:]], 1), tab, 0, 0)
    b = dot_r(cc([re[:, :h] - re[:, h:], im[:, :h] - im[:, h:]], 1), tab, 1, 0)
    re, im = cc([a[:, :h], b[:, :h]], 1), cc([a[:, h:], b[:, h:]], 1)
    a = dot_l(tab, 0, 1, cc([re[:h] + re[h:], im[:h] + im[h:]], 0))
    b = dot_l(tab, 1, 1, cc([re[:h] - re[h:], im[:h] - im[h:]], 0))
    return cc([a[:h], b[:h]], 0), cc([a[h:], b[h:]], 0)


def inverse_two(z, tab):
    re, im = z
    h = HALF
    a = dot_l(tab, 0, 0, cc([re[:h], im[:h]], 0))
    b = dot_l(tab, 1, 0, cc([re[h:], im[h:]], 0))
    s, d = a + b, a - b
    re, im = cc([s[:h], d[:h]], 0), cc([s[h:], d[h:]], 0)
    a = dot_r(cc([re[:, :h], im[:, :h]], 1), tab, 0, 1)
    b = dot_r(cc([re[:, h:], im[:, h:]], 1), tab, 1, 1)
    s, d = a + b, a - b
    return cc([s[:, :h], d[:, :h]], 1), cc([s[:, h:], d[:, h:]], 1)


def cmul(a, b):
    return a[0] * b[0] - a[1] * b[1], a[0] * b[1] + a[1] * b[0]


def cjmul(a, b):
    return a[0] * b[0] + a[1] * b[1], a[0] * b[1] - a[1] * b[0]


def place(r):
    base = pl.multiple_of(jnp.minimum(r // 8 * 8, EXT_R - WIN - 8), 8)
    return base, r - base


def lanes_left(x, c):
    keep = lax.broadcasted_iota(jnp.int32, (x.shape[0], HALF), 1) < HALF - c
    turn = lax.rem(HALF - c, HALF)
    a, b, d = [pltpu.roll(x[:, i * HALF : (i + 1) * HALF], turn, 1) for i in range(3)]
    return cc([jnp.where(keep, a, b), jnp.where(keep, b, d)], 1)


def lanes_right(x, c):
    keep = lax.broadcasted_iota(jnp.int32, (x.shape[0], HALF), 1) >= c
    turn = lax.rem(c, HALF)
    a, b = [pltpu.roll(x[:, i * HALF : (i + 1) * HALF], turn, 1) for i in range(2)]
    none = jnp.zeros_like(a)
    return cc([jnp.where(keep, a, none), jnp.where(keep, b, a), jnp.where(keep, none, b)], 1)


def rows_up(x, shift):
    y = x.reshape(WIN // 8 + 1, 8, x.shape[1])
    y = pltpu.roll(y, lax.rem(8 - shift, 8), 1)
    keep = lax.broadcasted_iota(jnp.int32, (WIN // 8, 8, x.shape[1]), 1) < 8 - shift
    return jnp.where(keep, y[:-1], y[1:]).reshape(WIN, x.shape[1])


def rows_down(x, shift):
    y = x.reshape(WIN // 8, 8, x.shape[1])
    y = pltpu.roll(y, lax.rem(shift, 8), 1)
    none = jnp.zeros((1, 8, x.shape[1]), f32)
    keep = lax.broadcasted_iota(jnp.int32, (WIN // 8 + 1, 8, x.shape[1]), 1) >= shift
    return jnp.where(keep, cc([y, none], 0), cc([none, y], 0)).reshape(WIN + 8, x.shape[1])


def load_window(ref, first, r, c):
    base, shift = place(r)
    out = []
    for p in (first, first + 1):
        t = lanes_left(ref[p, pl.ds(base, WIN + 8), :], c)
        out.append(rows_up(t, shift))
    return out


def add_window(ref, first, r, c, g):
    base, shift = place(r)
    for p in (first, first + 1):
        t = lanes_right(rows_down(g[p - first], shift), c)
        ref[p, pl.ds(base, WIN + 8), :] = ref[p, pl.ds(base, WIN + 8), :] + t


def reorder(x, order):
    a = x.astype(bf16)
    rest = x - a.astype(f32)
    b = rest.astype(bf16)
    c = (rest - b.astype(f32)).astype(bf16)
    m = order[0]
    y = jnp.dot(a, m, preferred_element_type=f32)
    y = y + jnp.dot(b, m, preferred_element_type=f32)
    y = y + jnp.dot(c, m, preferred_element_type=f32)
    a = y.astype(bf16)
    rest = y - a.astype(f32)
    b = rest.astype(bf16)
    c = (rest - b.astype(f32)).astype(bf16)
    m = order[1]
    y = jnp.dot(m, a, preferred_element_type=f32)
    y = y + jnp.dot(m, b, preferred_element_type=f32)
    return y + jnp.dot(m, c, preferred_element_type=f32)


def prep_kernel(amp, phase, order, amp_out, prop_out):
    def step(s, _):
        amp_out[s] = reorder(amp[0, 0, s], order)
        return 0

    lax.fori_loop(0, SLOTS, step, 0)
    ph = reorder(phase[...], order)
    prop_out[0] = jnp.cos(ph)
    prop_out[1] = jnp.sin(ph)


def inside(axis):
    return lax.axis_index(axis) < lax.axis_size(axis) - 1


def assemble_kernel(main, right_top, right_rest, bottom, *rest):
    state = rest[-1]
    first = 0 if len(rest) == 1 else 2
    for k in range(2):
        p = first + k
        state[p, :ROWS, :COLS] = main[first // 2, k]
        state[p, :HALF, COLS:] = right_top[p]
        state[p, HALF:ROWS, COLS:] = right_rest[k]
        state[p, ROWS:, :] = bottom[p]


def fold_sides(old, state, mid_l, mid_r, end_l, end_r, core):
    scale = jnp.where(inside("col"), 0.5, 0.0).astype(f32)
    drop = jnp.where(inside("row"), 1.0, 0.0).astype(f32)
    for p in range(4):
        for cols, fac, mid, end in (
            (pl.ds(0, HALF), jnp.float32(0.5), mid_l, end_l),
            (pl.ds(COLS, HALF), scale, mid_r, end_r),
        ):
            state[p, :HALF, cols] = old[p, :HALF, cols] - fac * end[p, :HALF]
            state[p, HALF:ROWS, cols] = old[p, HALF:ROWS, cols] - fac * mid[p]
            state[p, ROWS:, cols] = old[p, ROWS:, cols] - (fac * drop) * end[p, HALF:]
        cols = pl.ds(HALF, HALF)
        state[p, ROWS:, cols] = old[p, ROWS:, cols] - (0.5 * drop) * core[p]


def windows(batch, stages, count, orow, ocol, wbatch, tab, probe, prop, amp, state, grad, between, mid):
    def step(s, _):
        @pl.when((s < count[0, 0]) & (wbatch[0, 0, s] == batch))
        def _():
            r = orow[0, 0, s]
            c = ocol[0, 0, s]
            if "a" in stages:
                psi = cmul((probe[0], probe[1]), load_window(state, 0, r, c))
                f = forward_two(psi, tab)
                bt = inverse_two(cmul((prop[0], prop[1]), f), tab)
                if "b" not in stages:
                    between[s, 0] = bt[0]
                    between[s, 1] = bt[1]
            if "b" in stages:
                if "a" not in stages:
                    bt = (between[s, 0], between[s, 1])
                w2 = load_window(state, 2, r, c)
                far = forward_two(cmul(bt, w2), tab)
                power = far[0] * far[0] + far[1] * far[1]
                factor = 1.0 - amp[s] * lax.rsqrt(jnp.maximum(power, 1.0))
                back = inverse_two((far[0] * factor, far[1] * factor), tab)
                add_window(grad, 2, r, c, cjmul(bt, back))
                m = cjmul(w2, back)
                if "c" not in stages:
                    mid[s, 0] = m[0]
                    mid[s, 1] = m[1]
            if "c" in stages:
                if "b" not in stages:
                    m = (mid[s, 0], mid[s, 1])
                f = forward_two(m, tab)
                back = inverse_two(cjmul((prop[0], prop[1]), f), tab)
                add_window(grad, 0, r, c, cjmul((probe[0], probe[1]), back))

        return 0

    lax.fori_loop(0, SLOTS, step, 0)


def edges_of(grad, side_l, side_r, top, top_core, bottom):
    side_l[...] = grad[:, HALF:ROWS, :HALF]
    side_r[...] = grad[:, HALF:ROWS, COLS:]
    top[:, :, :HALF] = grad[:, :HALF, :HALF]
    top[:, :, HALF:] = grad[:, :HALF, COLS:]
    top_core[...] = grad[:, :HALF, HALF:COLS]
    bottom[...] = grad[:, ROWS:, :]


def early_kernel(count, orow, ocol, wbatch, tab, probe, prop, state, between):
    windows(0, "a", count, orow, ocol, wbatch, tab, probe, prop, None, state, None, between, None)


def first_kernel(count, orow, ocol, wbatch, tab, probe, prop, amp, state, between, grad, *out):
    grad[...] = jnp.zeros_like(grad)
    windows(0, "bc", count, orow, ocol, wbatch, tab, probe, prop, amp, state, grad, between, None)
    edges_of(grad, *out)


def batch_kernel(batch):
    def run(count, orow, ocol, wbatch, tab, probe, prop, amp, old, *rest):
        sides, (state, grad), out = rest[:5], rest[5:7], rest[7:]
        fold_sides(old, state, *sides)
        grad[...] = jnp.zeros_like(grad)
        windows(batch, "abc", count, orow, ocol, wbatch, tab, probe, prop, amp, state, grad, None, None)
        edges_of(grad, *out)

    return run


def final_kernel(count, orow, ocol, wbatch, tab, probe, prop, amp, old, *rest):
    sides, (state, grad, mid, side_r) = rest[:5], rest[5:]
    fold_sides(old, state, *sides)
    grad[...] = jnp.zeros_like(grad)
    windows(BATCHES - 1, "ab", count, orow, ocol, wbatch, tab, probe, prop, amp, state, grad, None, mid)
    side_r[...] = grad[2:, HALF:ROWS, COLS:]


def late_kernel(count, orow, ocol, wbatch, tab, probe, prop, mid, old, grad, side_r, corner, low):
    windows(BATCHES - 1, "c", count, orow, ocol, wbatch, tab, probe, prop, None, None, grad, None, mid)
    side_r[...] = grad[:2, HALF:ROWS, COLS:]
    corner[...] = grad[:, ROWS:, COLS:]
    low[...] = grad[:, ROWS:, :COLS]


def settle_kernel(state, grad, above, below, out, end_l, end_r):
    in_r = jnp.where(inside("row"), 0.5, 0.0).astype(f32)
    in_c = jnp.where(inside("col"), 1.0, 0.0).astype(f32)
    h = HALF
    for p in range(4):
        for at, near, ends in ((0, above, pl.ds(0, h)), (h, None, None), (ROWS, below, pl.ds(h, h))):
            rows = pl.ds(at, ROWS - h if near is None else h)
            left, mid, right = grad[p, rows, :h], grad[p, rows, h:COLS], grad[p, rows, COLS:]
            if near is not None:
                left = left + near[p, :, :h]
                right = right + near[p, :, -h:]
                if at == 0:
                    mid = mid + near[p, :, h:COLS]
                end_l[p, ends] = left
                end_r[p, ends] = right
            scale = in_r if at == ROWS else jnp.float32(0.5)
            out[p, rows, :h] = state[p, rows, :h] - scale * left
            out[p, rows, h:COLS] = state[p, rows, h:COLS] - scale * mid
            out[p, rows, COLS:] = state[p, rows, COLS:] - (scale * in_c) * right


def final_settle_kernel(state, grad, corner, out, end_r):
    for p in range(4):
        end_r[p] = grad[p, :HALF, COLS:] + corner[p]
        out[p] = state[p, :ROWS, :COLS] - 0.5 * grad[p, :ROWS, :COLS]


def last_kernel(state, mid1, mid2, end, low, out):
    h = HALF
    for p in range(4):
        q = (p // 2, p % 2)
        mid = (mid1, mid2)[p // 2]
        out[(*q, slice(0, h), slice(0, h))] = state[p, :h, :h] - 0.5 * (end[p] + low[p, :, :h])
        out[(*q, slice(h, ROWS), slice(0, h))] = state[p, h:, :h] - 0.5 * mid[p % 2]
        out[(*q, slice(0, h), slice(h, COLS))] = state[p, :h, h:] - 0.5 * low[p, :, h:]
        out[(*q, slice(h, ROWS), slice(h, COLS))] = state[p, h:, h:]


VM = pl.BlockSpec(memory_space=pltpu.VMEM)
SM = pl.BlockSpec(memory_space=pltpu.SMEM)
EXT = (4, EXT_R, EXT_C)
EDGE = (4, HALF, 2 * HALF)
CORE = (4, HALF, HALF)
FLAT = (4, HALF, EXT_C)
SIDE = (2, ROWS - HALF, HALF)
PLANES = (SLOTS, 2, WIN, WIN)
MIDS = (4, ROWS - HALF, HALF)
ENDS = (4, 2 * HALF, HALF)


def call(kernel, scalars, arrays, outs, alias=None, limit=24):
    return pl.pallas_call(
        kernel,
        in_specs=[SM] * len(scalars) + [VM] * len(arrays),
        out_specs=[VM] * len(outs),
        out_shape=[jax.ShapeDtypeStruct(s, f32) for s in outs],
        input_output_aliases=alias or {},
        compiler_params=pltpu.CompilerParams(vmem_limit_bytes=limit * 2**20),
    )(*scalars, *arrays)


def from_behind(array, axis, by):
    size = lax.axis_size(axis)
    pairs = [(i, i + by) for i in range(size) if 0 <= i + by < size]
    return lax.ppermute(array, axis, pairs)


def body(transmission, probe, phase, amplitude, count, orow, ocol, wbatch):
    tab = jnp.asarray(dft_tables())
    order = jnp.asarray(order_matrix())
    scalars = (count, orow, ocol, wbatch)
    h = HALF
    planes = transmission.reshape(4, ROWS, COLS)
    right_top = from_behind(planes[:, :h, :h], "col", -1)
    right_1 = from_behind(planes[:2, h:, :h], "col", -1)
    right_2 = from_behind(planes[2:, h:, :h], "col", -1)
    amp, prop = call(prep_kernel, (), (amplitude, phase, order), [(SLOTS, WIN, WIN), (2, WIN, WIN)])
    low = cc([planes[:, :h, :], right_top], 2)
    bottom = from_behind(low, "row", -1)
    (state,) = call(assemble_kernel, (), (transmission, right_top, right_1, bottom), [EXT])
    (between,) = call(early_kernel, scalars, (tab, probe, prop, state), [PLANES])
    (state,) = call(
        assemble_kernel, (), (transmission, right_top, right_2, bottom, state), [EXT], {4: 0}
    )
    edges = [MIDS, MIDS, EDGE, CORE, FLAT]
    for b in range(BATCHES - 1):
        common = (tab, probe, prop, amp, state)
        if b == 0:
            grad, *sent = call(first_kernel, scalars, (*common, between), [EXT, *edges])
        else:
            state, grad, *sent = call(
                batch_kernel(b), scalars, (*common, *parts), [EXT, EXT, *edges], {8: 0}
            )
        side_l, side_r, top, top_core, bottom = sent
        mid_l = from_behind(side_r, "col", 1)
        mid_r = from_behind(side_l, "col", -1)
        above = from_behind(bottom, "row", 1)
        below = from_behind(top, "row", -1)
        core = from_behind(top_core, "row", -1)
        state, end_l, end_r = call(
            settle_kernel, (), (state, grad, above, below), [EXT, ENDS, ENDS], {0: 0}
        )
        parts = (mid_l, mid_r, from_behind(end_r, "col", 1), from_behind(end_l, "col", -1), core)
    state, grad, mid, side_2 = call(
        final_kernel,
        scalars,
        (tab, probe, prop, amp, state, *parts),
        [EXT, EXT, PLANES, SIDE],
        {8: 0},
    )
    mid_2 = from_behind(side_2, "col", 1)
    grad, side_1, corner, low = call(
        late_kernel, scalars, (tab, probe, prop, mid, grad), [EXT, SIDE, CORE, EDGE], {8: 0}
    )
    mid_1 = from_behind(side_1, "col", 1)
    corner = from_behind(corner, "row", 1)
    main, end_r = call(final_settle_kernel, (), (state, grad, corner), [(4, ROWS, COLS), CORE])
    end = from_behind(end_r, "col", 1)
    low = from_behind(low, "row", 1)
    return call(last_kernel, (), (main, mid_1, mid_2, end, low), [(2, 2, ROWS, COLS)])[0]


def solution(mesh):
    in_specs = (
        P(None, None, "row", "col"),
        P(),
        P(),
        P("row", "col", None, None, None),
        P("row", "col"),
        P("row", "col", None),
        P("row", "col", None),
        P("row", "col", None),
    )
    out_specs = P(None, None, "row", "col")
    return jax.shard_map(body, mesh=mesh, in_specs=in_specs, out_specs=out_specs, check_vma=False)
```

```python
import math

import jax
import jax.numpy as jnp
import numpy as np
from jax import lax
from jax.experimental import pallas as pl
from jax.experimental.pallas import tpu as pltpu
from jax.sharding import PartitionSpec as P

BATCHES = 3
WIN = 256
HALF = 128
SLOTS = 4
ROWS = 512
COLS = 256
EXT_R = 640
EXT_C = 384


cc = jnp.concatenate
f32 = jnp.float32
bf16 = jnp.bfloat16


def dft_tables():
    n = np.arange(HALF)
    even = np.exp(-2j * np.pi * (np.outer(n, n) % HALF) / HALF) / math.sqrt(WIN)
    odd = np.exp(-2j * np.pi * n / WIN)[:, None] * even
    out = []
    for m in (even, odd):
        full = np.block([[m.real, m.imag], [-m.imag, m.real]]).astype(np.float32)
        for t in (full, full.T):
            hi = t.astype(bf16)
            lo = (t - hi.astype(np.float32)).astype(bf16)
            out.append(np.stack([hi, lo]))
    return np.stack(out).reshape(2, 2, 2, WIN, WIN)


def order_matrix():
    source = np.concatenate([np.arange(0, WIN, 2), np.arange(1, WIN, 2)])
    m = np.zeros((WIN, WIN), np.float32)
    m[source, np.arange(WIN)] = 1.0
    return np.stack([m, m.T]).astype(bf16)


def halves(x):
    hi = x.astype(bf16)
    lo = (x - hi.astype(f32)).astype(bf16)
    return hi, lo


def dot_r(x, tab, which, trans):
    hi, lo = halves(x)
    th = tab[which, trans, 0]
    t = cc([th, th, tab[which, trans, 1]], 0)
    return jnp.dot(cc([hi, lo, hi], 1), t, preferred_element_type=f32)


def dot_l(tab, which, trans, x):
    hi, lo = halves(x)
    th = tab[which, trans, 0]
    t = cc([th, th, tab[which, trans, 1]], 1)
    return jnp.dot(t, cc([hi, lo, hi], 0), preferred_element_type=f32)


def forward_two(z, tab):
    re, im = z
    h = HALF
    a = dot_r(cc([re[:, :h] + re[:, h:], im[:, :h] + im[:, h:]], 1), tab, 0, 0)
    b = dot_r(cc([re[:, :h] - re[:, h:], im[:, :h] - im[:, h:]], 1), tab, 1, 0)
    re, im = cc([a[:, :h], b[:, :h]], 1), cc([a[:, h:], b[:, h:]], 1)
    a = dot_l(tab, 0, 1, cc([re[:h] + re[h:], im[:h] + im[h:]], 0))
    b = dot_l(tab, 1, 1, cc([re[:h] - re[h:], im[:h] - im[h:]], 0))
    return cc([a[:h], b[:h]], 0), cc([a[h:], b[h:]], 0)


def inverse_two(z, tab):
    re, im = z
    h = HALF
    a = dot_l(tab, 0, 0, cc([re[:h], im[:h]], 0))
    b = dot_l(tab, 1, 0, cc([re[h:], im[h:]], 0))
    s, d = a + b, a - b
    re, im = cc([s[:h], d[:h]], 0), cc([s[h:], d[h:]], 0)
    a = dot_r(cc([re[:, :h], im[:, :h]], 1), tab, 0, 1)
    b = dot_r(cc([re[:, h:], im[:, h:]], 1), tab, 1, 1)
    s, d = a + b, a - b
    return cc([s[:, :h], d[:, :h]], 1), cc([s[:, h:], d[:, h:]], 1)


def cmul(a, b):
    return a[0] * b[0] - a[1] * b[1], a[0] * b[1] + a[1] * b[0]


def cjmul(a, b):
    return a[0] * b[0] + a[1] * b[1], a[0] * b[1] - a[1] * b[0]


def place(r):
    base = pl.multiple_of(jnp.minimum(r // 8 * 8, EXT_R - WIN - 8), 8)
    return base, r - base


def lanes_left(x, c):
    keep = lax.broadcasted_iota(jnp.int32, (x.shape[0], HALF), 1) < HALF - c
    turn = lax.rem(HALF - c, HALF)
    a, b, d = [pltpu.roll(x[:, i * HALF : (i + 1) * HALF], turn, 1) for i in range(3)]
    return cc([jnp.where(keep, a, b), jnp.where(keep, b, d)], 1)


def lanes_right(x, c):
    keep = lax.broadcasted_iota(jnp.int32, (x.shape[0], HALF), 1) >= c
    turn = lax.rem(c, HALF)
    a, b = [pltpu.roll(x[:, i * HALF : (i + 1) * HALF], turn, 1) for i in range(2)]
    none = jnp.zeros_like(a)
    return cc([jnp.where(keep, a, none), jnp.where(keep, b, a), jnp.where(keep, none, b)], 1)


def rows_up(x, shift):
    y = x.reshape(WIN // 8 + 1, 8, x.shape[1])
    y = pltpu.roll(y, lax.rem(8 - shift, 8), 1)
    keep = lax.broadcasted_iota(jnp.int32, (WIN // 8, 8, x.shape[1]), 1) < 8 - shift
    return jnp.where(keep, y[:-1], y[1:]).reshape(WIN, x.shape[1])


def rows_down(x, shift):
    y = x.reshape(WIN // 8, 8, x.shape[1])
    y = pltpu.roll(y, lax.rem(shift, 8), 1)
    none = jnp.zeros((1, 8, x.shape[1]), f32)
    keep = lax.broadcasted_iota(jnp.int32, (WIN // 8 + 1, 8, x.shape[1]), 1) >= shift
    return jnp.where(keep, cc([y, none], 0), cc([none, y], 0)).reshape(WIN + 8, x.shape[1])


def load_window(ref, first, r, c):
    base, shift = place(r)
    out = []
    for p in (first, first + 1):
        t = lanes_left(ref[p, pl.ds(base, WIN + 8), :], c)
        out.append(rows_up(t, shift))
    return out


def add_window(ref, first, r, c, g):
    base, shift = place(r)
    for p in (first, first + 1):
        t = lanes_right(rows_down(g[p - first], shift), c)
        ref[p, pl.ds(base, WIN + 8), :] = ref[p, pl.ds(base, WIN + 8), :] + t


def reorder(x, order):
    a = x.astype(bf16)
    rest = x - a.astype(f32)
    b = rest.astype(bf16)
    c = (rest - b.astype(f32)).astype(bf16)
    m = order[0]
    y = jnp.dot(a, m, preferred_element_type=f32)
    y = y + jnp.dot(b, m, preferred_element_type=f32)
    y = y + jnp.dot(c, m, preferred_element_type=f32)
    a = y.astype(bf16)
    rest = y - a.astype(f32)
    b = rest.astype(bf16)
    c = (rest - b.astype(f32)).astype(bf16)
    m = order[1]
    y = jnp.dot(m, a, preferred_element_type=f32)
    y = y + jnp.dot(m, b, preferred_element_type=f32)
    return y + jnp.dot(m, c, preferred_element_type=f32)


def prep_kernel(amp, phase, order, amp_out, prop_out):
    def step(s, _):
        amp_out[s] = reorder(amp[0, 0, s], order)
        return 0

    lax.fori_loop(0, SLOTS, step, 0)
    ph = reorder(phase[...], order)
    prop_out[0] = jnp.cos(ph)
    prop_out[1] = jnp.sin(ph)


def inside(axis):
    return lax.axis_index(axis) < lax.axis_size(axis) - 1


def assemble_kernel(main, right_top, right_rest, bottom, *rest):
    state = rest[-1]
    first = 0 if len(rest) == 1 else 2
    for k in range(2):
        p = first + k
        state[p, :ROWS, :COLS] = main[first // 2, k]
        state[p, :HALF, COLS:] = right_top[p]
        state[p, HALF:ROWS, COLS:] = right_rest[k]
        state[p, ROWS:, :] = bottom[p]


def fold_sides(old, state, mid_l, mid_r, above, below):
    in_c = jnp.where(inside("col"), 1.0, 0.0).astype(f32)
    in_r = jnp.where(inside("row"), 1.0, 0.0).astype(f32)
    rows = pl.ds(HALF, ROWS - HALF)
    for p in range(4):
        state[p, rows, :HALF] = old[p, rows, :HALF] - 0.5 * mid_l[p]
        state[p, rows, COLS:] = old[p, rows, COLS:] - (0.5 * in_c) * mid_r[p]
        for at, fac, near in ((pl.ds(0, HALF), 0.5, above), (pl.ds(ROWS, HALF), 0.5 * in_r, below)):
            state[p, at, :COLS] = old[p, at, :COLS] - fac * near[p, :, :COLS]
            state[p, at, COLS:] = old[p, at, COLS:] - (fac * in_c) * near[p, :, COLS:]


def windows(batch, stages, count, orow, ocol, wbatch, tab, probe, prop, amp, state, grad, between, mid):
    def step(s, _):
        @pl.when((s < count[0, 0]) & (wbatch[0, 0, s] == batch))
        def _():
            r = orow[0, 0, s]
            c = ocol[0, 0, s]
            if "a" in stages:
                psi = cmul((probe[0], probe[1]), load_window(state, 0, r, c))
                f = forward_two(psi, tab)
                bt = inverse_two(cmul((prop[0], prop[1]), f), tab)
                if "b" not in stages:
                    between[s, 0] = bt[0]
                    between[s, 1] = bt[1]
            if "b" in stages:
                if "a" not in stages:
                    bt = (between[s, 0], between[s, 1])
                w2 = load_window(state, 2, r, c)
                far = forward_two(cmul(bt, w2), tab)
                power = far[0] * far[0] + far[1] * far[1]
                factor = 1.0 - amp[s] * lax.rsqrt(jnp.maximum(power, 1.0))
                back = inverse_two((far[0] * factor, far[1] * factor), tab)
                add_window(grad, 2, r, c, cjmul(bt, back))
                m = cjmul(w2, back)
                if "c" not in stages:
                    mid[s, 0] = m[0]
                    mid[s, 1] = m[1]
            if "c" in stages:
                if "b" not in stages:
                    m = (mid[s, 0], mid[s, 1])
                f = forward_two(m, tab)
                back = inverse_two(cjmul((prop[0], prop[1]), f), tab)
                add_window(grad, 0, r, c, cjmul((probe[0], probe[1]), back))

        return 0

    lax.fori_loop(0, SLOTS, step, 0)


def edges_of(grad, mid_l, mid_r, end_l, end_r):
    for mid, end, cols in ((mid_l, end_l, pl.ds(0, HALF)), (mid_r, end_r, pl.ds(COLS, HALF))):
        mid[...] = grad[:, HALF:ROWS, cols]
        end[:, :HALF, :] = grad[:, :HALF, cols]
        end[:, HALF:, :] = grad[:, ROWS:, cols]


def early_kernel(count, orow, ocol, wbatch, tab, probe, prop, state, between):
    windows(0, "a", count, orow, ocol, wbatch, tab, probe, prop, None, state, None, between, None)


def first_kernel(count, orow, ocol, wbatch, tab, probe, prop, amp, state, between, grad, *out):
    grad[...] = jnp.zeros_like(grad)
    windows(0, "bc", count, orow, ocol, wbatch, tab, probe, prop, amp, state, grad, between, None)
    edges_of(grad, *out)


def batch_kernel(batch):
    def run(count, orow, ocol, wbatch, tab, probe, prop, amp, old, *rest):
        sides, (state, grad), out = rest[:4], rest[4:6], rest[6:]
        fold_sides(old, state, *sides)
        grad[...] = jnp.zeros_like(grad)
        windows(batch, "abc", count, orow, ocol, wbatch, tab, probe, prop, amp, state, grad, None, None)
        edges_of(grad, *out)

    return run


def final_kernel(count, orow, ocol, wbatch, tab, probe, prop, amp, old, *rest):
    sides, (state, grad, mid, side_r) = rest[:4], rest[4:]
    fold_sides(old, state, *sides)
    grad[...] = jnp.zeros_like(grad)
    windows(BATCHES - 1, "ab", count, orow, ocol, wbatch, tab, probe, prop, amp, state, grad, None, mid)
    side_r[...] = grad[2:, HALF:ROWS, COLS:]


def late_kernel(count, orow, ocol, wbatch, tab, probe, prop, mid, old, grad, side_r, corner, low):
    windows(BATCHES - 1, "c", count, orow, ocol, wbatch, tab, probe, prop, None, None, grad, None, mid)
    side_r[...] = grad[:2, HALF:ROWS, COLS:]
    corner[...] = grad[:, ROWS:, COLS:]
    low[...] = grad[:, ROWS:, :COLS]


def settle_kernel(state, grad, end_l, end_r, out, top, bottom):
    in_r = jnp.where(inside("row"), 0.5, 0.0).astype(f32)
    in_c = jnp.where(inside("col"), 1.0, 0.0).astype(f32)
    h = HALF
    for p in range(4):
        for at, flat, ends in ((0, top, pl.ds(0, h)), (h, None, None), (ROWS, bottom, pl.ds(h, h))):
            rows = pl.ds(at, ROWS - h if flat is None else h)
            left, mid, right = grad[p, rows, :h], grad[p, rows, h:COLS], grad[p, rows, COLS:]
            if flat is not None:
                left = left + end_l[p, ends]
                right = right + end_r[p, ends]
                flat[p, :, :h] = left
                flat[p, :, h:COLS] = mid
                flat[p, :, COLS:] = right
            scale = in_r if at == ROWS else jnp.float32(0.5)
            out[p, rows, :h] = state[p, rows, :h] - scale * left
            out[p, rows, h:COLS] = state[p, rows, h:COLS] - scale * mid
            out[p, rows, COLS:] = state[p, rows, COLS:] - (scale * in_c) * right


def final_settle_kernel(state, grad, corner, out, end_r):
    for p in range(4):
        end_r[p] = grad[p, :HALF, COLS:] + corner[p]
        out[p] = state[p, :ROWS, :COLS] - 0.5 * grad[p, :ROWS, :COLS]


def last_kernel(state, mid1, mid2, end, low, out):
    h = HALF
    for p in range(4):
        q = (p // 2, p % 2)
        mid = (mid1, mid2)[p // 2]
        out[(*q, slice(0, h), slice(0, h))] = state[p, :h, :h] - 0.5 * (end[p] + low[p, :, :h])
        out[(*q, slice(h, ROWS), slice(0, h))] = state[p, h:, :h] - 0.5 * mid[p % 2]
        out[(*q, slice(0, h), slice(h, COLS))] = state[p, :h, h:] - 0.5 * low[p, :, h:]
        out[(*q, slice(h, ROWS), slice(h, COLS))] = state[p, h:, h:]


VM = pl.BlockSpec(memory_space=pltpu.VMEM)
SM = pl.BlockSpec(memory_space=pltpu.SMEM)
EXT = (4, EXT_R, EXT_C)
EDGE = (4, HALF, 2 * HALF)
CORE = (4, HALF, HALF)
FLAT = (4, HALF, EXT_C)
SIDE = (2, ROWS - HALF, HALF)
PLANES = (SLOTS, 2, WIN, WIN)
MIDS = (4, ROWS - HALF, HALF)
ENDS = (4, 2 * HALF, HALF)


def call(kernel, scalars, arrays, outs, alias=None, limit=24):
    return pl.pallas_call(
        kernel,
        in_specs=[SM] * len(scalars) + [VM] * len(arrays),
        out_specs=[VM] * len(outs),
        out_shape=[jax.ShapeDtypeStruct(s, f32) for s in outs],
        input_output_aliases=alias or {},
        compiler_params=pltpu.CompilerParams(vmem_limit_bytes=limit * 2**20),
    )(*scalars, *arrays)


def from_behind(array, axis, by):
    size = lax.axis_size(axis)
    pairs = [(i, i + by) for i in range(size) if 0 <= i + by < size]
    return lax.ppermute(array, axis, pairs)


def body(transmission, probe, phase, amplitude, count, orow, ocol, wbatch):
    tab = jnp.asarray(dft_tables())
    order = jnp.asarray(order_matrix())
    scalars = (count, orow, ocol, wbatch)
    h = HALF
    planes = transmission.reshape(4, ROWS, COLS)
    right_top = from_behind(planes[:, :h, :h], "col", -1)
    right_1 = from_behind(planes[:2, h:, :h], "col", -1)
    right_2 = from_behind(planes[2:, h:, :h], "col", -1)
    amp, prop = call(prep_kernel, (), (amplitude, phase, order), [(SLOTS, WIN, WIN), (2, WIN, WIN)])
    low = cc([planes[:, :h, :], right_top], 2)
    bottom = from_behind(low, "row", -1)
    (state,) = call(assemble_kernel, (), (transmission, right_top, right_1, bottom), [EXT])
    (between,) = call(early_kernel, scalars, (tab, probe, prop, state), [PLANES])
    (state,) = call(
        assemble_kernel, (), (transmission, right_top, right_2, bottom, state), [EXT], {4: 0}
    )
    edges = [MIDS, MIDS, ENDS, ENDS]
    for b in range(BATCHES - 1):
        common = (tab, probe, prop, amp, state)
        if b == 0:
            grad, *sent = call(first_kernel, scalars, (*common, between), [EXT, *edges])
        else:
            state, grad, *sent = call(
                batch_kernel(b), scalars, (*common, *parts), [EXT, EXT, *edges], {8: 0}
            )
        mid_l, mid_r, end_l, end_r = sent
        from_left = from_behind(end_r, "col", 1)
        from_right = from_behind(end_l, "col", -1)
        mid_left = from_behind(mid_r, "col", 1)
        mid_right = from_behind(mid_l, "col", -1)
        state, top, bottom = call(
            settle_kernel, (), (state, grad, from_left, from_right), [EXT, FLAT, FLAT], {0: 0}
        )
        parts = (mid_left, mid_right, from_behind(bottom, "row", 1), from_behind(top, "row", -1))
    state, grad, mid, side_2 = call(
        final_kernel,
        scalars,
        (tab, probe, prop, amp, state, *parts),
        [EXT, EXT, PLANES, SIDE],
        {8: 0},
    )
    mid_2 = from_behind(side_2, "col", 1)
    grad, side_1, corner, low = call(
        late_kernel, scalars, (tab, probe, prop, mid, grad), [EXT, SIDE, CORE, EDGE], {8: 0}
    )
    mid_1 = from_behind(side_1, "col", 1)
    corner = from_behind(corner, "row", 1)
    low = from_behind(low, "row", 1)
    main, end_r = call(final_settle_kernel, (), (state, grad, corner), [(4, ROWS, COLS), CORE])
    end = from_behind(end_r, "col", 1)
    return call(last_kernel, (), (main, mid_1, mid_2, end, low), [(2, 2, ROWS, COLS)])[0]


def solution(mesh):
    in_specs = (
        P(None, None, "row", "col"),
        P(),
        P(),
        P("row", "col", None, None, None),
        P("row", "col"),
        P("row", "col", None),
        P("row", "col", None),
        P("row", "col", None),
    )
    out_specs = P(None, None, "row", "col")
    return jax.shard_map(body, mesh=mesh, in_specs=in_specs, out_specs=out_specs, check_vma=False)
```

```python
import math

import jax
import jax.numpy as jnp
import numpy as np
from jax import lax
from jax.experimental import pallas as pl
from jax.experimental.pallas import tpu as pltpu
from jax.sharding import PartitionSpec as P

BATCHES = 3
WIN = 256
HALF = 128
SLOTS = 4
ROWS = 512
COLS = 256
EXT_R = 640
EXT_C = 384


cc = jnp.concatenate
f32 = jnp.float32
bf16 = jnp.bfloat16


def dft_tables():
    n = np.arange(HALF)
    even = np.exp(-2j * np.pi * (np.outer(n, n) % HALF) / HALF) / math.sqrt(WIN)
    odd = np.exp(-2j * np.pi * n / WIN)[:, None] * even
    out = []
    for m in (even, odd):
        full = np.block([[m.real, m.imag], [-m.imag, m.real]]).astype(np.float32)
        for t in (full, full.T):
            hi = t.astype(bf16)
            lo = (t - hi.astype(np.float32)).astype(bf16)
            out.append(np.stack([hi, lo]))
    return np.stack(out).reshape(2, 2, 2, WIN, WIN)


def order_matrices():
    rows = lax.broadcasted_iota(jnp.int32, (WIN, WIN), 0)
    cols = lax.broadcasted_iota(jnp.int32, (WIN, WIN), 1)

    def source(k):
        return jnp.where(k < HALF, 2 * k, 2 * k - (WIN - 1))

    one, none = jnp.float32(1.0), jnp.float32(0.0)
    return [
        jnp.where(rows == source(cols), one, none).astype(bf16),
        jnp.where(cols == source(rows), one, none).astype(bf16),
    ]


def halves(x):
    hi = x.astype(bf16)
    lo = (x - hi.astype(f32)).astype(bf16)
    return hi, lo


PAIRED = [b for i in range(8) for b in (i, i + 8)]
NATURAL = [PAIRED.index(b) for b in range(16)]


def blocks(x, order):
    return cc([x[16 * b : 16 * b + 16] for b in order], 0)


def dot_r(x, tab, which, trans):
    hi, lo = halves(blocks(x, PAIRED))
    th = tab[which, trans, 0]
    t = cc([th, th, tab[which, trans, 1]], 0)
    return blocks(jnp.dot(cc([hi, lo, hi], 1), t, preferred_element_type=f32), NATURAL)


def dot_l(tab, which, trans, x):
    hi, lo = halves(x)
    th = tab[which, trans, 0]
    t = blocks(cc([th, th, tab[which, trans, 1]], 1), PAIRED)
    return blocks(jnp.dot(t, cc([hi, lo, hi], 0), preferred_element_type=f32), NATURAL)


def forward_two(z, tab):
    re, im = z
    h = HALF
    a = dot_r(cc([re[:, :h] + re[:, h:], im[:, :h] + im[:, h:]], 1), tab, 0, 0)
    b = dot_r(cc([re[:, :h] - re[:, h:], im[:, :h] - im[:, h:]], 1), tab, 1, 0)
    re, im = cc([a[:, :h], b[:, :h]], 1), cc([a[:, h:], b[:, h:]], 1)
    a = dot_l(tab, 0, 1, cc([re[:h] + re[h:], im[:h] + im[h:]], 0))
    b = dot_l(tab, 1, 1, cc([re[:h] - re[h:], im[:h] - im[h:]], 0))
    return cc([a[:h], b[:h]], 0), cc([a[h:], b[h:]], 0)


def inverse_two(z, tab):
    re, im = z
    h = HALF
    a = dot_l(tab, 0, 0, cc([re[:h], im[:h]], 0))
    b = dot_l(tab, 1, 0, cc([re[h:], im[h:]], 0))
    s, d = a + b, a - b
    re, im = cc([s[:h], d[:h]], 0), cc([s[h:], d[h:]], 0)
    a = dot_r(cc([re[:, :h], im[:, :h]], 1), tab, 0, 1)
    b = dot_r(cc([re[:, h:], im[:, h:]], 1), tab, 1, 1)
    s, d = a + b, a - b
    return cc([s[:, :h], d[:, :h]], 1), cc([s[:, h:], d[:, h:]], 1)


def cmul(a, b):
    return a[0] * b[0] - a[1] * b[1], a[0] * b[1] + a[1] * b[0]


def cjmul(a, b):
    return a[0] * b[0] + a[1] * b[1], a[0] * b[1] - a[1] * b[0]


def place(r):
    base = pl.multiple_of(jnp.minimum(r // 8 * 8, EXT_R - WIN - 8), 8)
    return base, r - base


def lanes_left(x, c):
    keep = lax.broadcasted_iota(jnp.int32, (x.shape[0], HALF), 1) < HALF - c
    turn = lax.rem(HALF - c, HALF)
    a, b, d = [pltpu.roll(x[:, i * HALF : (i + 1) * HALF], turn, 1) for i in range(3)]
    return cc([jnp.where(keep, a, b), jnp.where(keep, b, d)], 1)


def lanes_right(x, c):
    keep = lax.broadcasted_iota(jnp.int32, (x.shape[0], HALF), 1) >= c
    turn = lax.rem(c, HALF)
    a, b = [pltpu.roll(x[:, i * HALF : (i + 1) * HALF], turn, 1) for i in range(2)]
    none = jnp.zeros_like(a)
    return cc([jnp.where(keep, a, none), jnp.where(keep, b, a), jnp.where(keep, none, b)], 1)


def rows_up(x, shift):
    y = x.reshape(WIN // 8 + 1, 8, x.shape[1])
    y = pltpu.roll(y, lax.rem(8 - shift, 8), 1)
    keep = lax.broadcasted_iota(jnp.int32, (WIN // 8, 8, x.shape[1]), 1) < 8 - shift
    return jnp.where(keep, y[:-1], y[1:]).reshape(WIN, x.shape[1])


def rows_down(x, shift):
    y = x.reshape(WIN // 8, 8, x.shape[1])
    y = pltpu.roll(y, lax.rem(shift, 8), 1)
    none = jnp.zeros((1, 8, x.shape[1]), f32)
    keep = lax.broadcasted_iota(jnp.int32, (WIN // 8 + 1, 8, x.shape[1]), 1) >= shift
    return jnp.where(keep, cc([y, none], 0), cc([none, y], 0)).reshape(WIN + 8, x.shape[1])


def load_window(ref, first, r, c):
    base, shift = place(r)
    out = []
    for p in (first, first + 1):
        t = lanes_left(ref[p, pl.ds(base, WIN + 8), :], c)
        out.append(rows_up(t, shift))
    return out


def add_window(ref, first, r, c, g):
    base, shift = place(r)
    for p in (first, first + 1):
        t = lanes_right(rows_down(g[p - first], shift), c)
        ref[p, pl.ds(base, WIN + 8), :] = ref[p, pl.ds(base, WIN + 8), :] + t


def reorder(x, order):
    a = x.astype(bf16)
    rest = x - a.astype(f32)
    b = rest.astype(bf16)
    c = (rest - b.astype(f32)).astype(bf16)
    m = order[0]
    y = jnp.dot(a, m, preferred_element_type=f32)
    y = y + jnp.dot(b, m, preferred_element_type=f32)
    y = y + jnp.dot(c, m, preferred_element_type=f32)
    a = y.astype(bf16)
    rest = y - a.astype(f32)
    b = rest.astype(bf16)
    c = (rest - b.astype(f32)).astype(bf16)
    m = order[1]
    y = jnp.dot(m, a, preferred_element_type=f32)
    y = y + jnp.dot(m, b, preferred_element_type=f32)
    return y + jnp.dot(m, c, preferred_element_type=f32)


def prep_kernel(amp, phase, amp_out, prop_out, grad):
    grad[...] = jnp.zeros_like(grad)
    order = order_matrices()

    def step(s, _):
        amp_out[s] = reorder(amp[0, 0, s], order)
        return 0

    lax.fori_loop(0, SLOTS, step, 0)
    ph = reorder(phase[...], order)
    prop_out[0] = jnp.cos(ph)
    prop_out[1] = jnp.sin(ph)


def inside(axis):
    return lax.axis_index(axis) < lax.axis_size(axis) - 1


def assemble_kernel(main, right_top, right_rest, bottom, *rest):
    state = rest[-1]
    first = 0 if len(rest) == 1 else 2
    for k in range(2):
        p = first + k
        state[p, :ROWS, :COLS] = main[first // 2, k]
        state[p, :HALF, COLS:] = right_top[p]
        state[p, HALF:ROWS, COLS:] = right_rest[k]
        state[p, ROWS:, :] = bottom[p]


def fold_sides(old, state, mid_l, mid_r, above, below):
    in_c = jnp.where(inside("col"), 1.0, 0.0).astype(f32)
    in_r = jnp.where(inside("row"), 1.0, 0.0).astype(f32)
    rows = pl.ds(HALF, ROWS - HALF)
    for p in range(4):
        state[p, rows, :HALF] = old[p, rows, :HALF] - 0.5 * mid_l[p]
        state[p, rows, COLS:] = old[p, rows, COLS:] - (0.5 * in_c) * mid_r[p]
        for at, fac, near in ((pl.ds(0, HALF), 0.5, above), (pl.ds(ROWS, HALF), 0.5 * in_r, below)):
            state[p, at, :COLS] = old[p, at, :COLS] - fac * near[p, :, :COLS]
            state[p, at, COLS:] = old[p, at, COLS:] - (fac * in_c) * near[p, :, COLS:]


def windows(batch, stages, count, orow, ocol, wbatch, tab, probe, prop, amp, state, grad, between, mid):
    def step(s, _):
        @pl.when((s < count[0, 0]) & (wbatch[0, 0, s] == batch))
        def _():
            r = orow[0, 0, s]
            c = ocol[0, 0, s]
            if "a" in stages:
                psi = cmul((probe[0], probe[1]), load_window(state, 0, r, c))
                f = forward_two(psi, tab)
                bt = inverse_two(cmul((prop[0], prop[1]), f), tab)
                if "b" not in stages:
                    between[s, 0] = bt[0]
                    between[s, 1] = bt[1]
            if "b" in stages:
                if "a" not in stages:
                    bt = (between[s, 0], between[s, 1])
                w2 = load_window(state, 2, r, c)
                far = forward_two(cmul(bt, w2), tab)
                power = far[0] * far[0] + far[1] * far[1]
                factor = 1.0 - amp[s] * lax.rsqrt(jnp.maximum(power, 1.0))
                back = inverse_two((far[0] * factor, far[1] * factor), tab)
                add_window(grad, 2, r, c, cjmul(bt, back))
                m = cjmul(w2, back)
                if "c" not in stages:
                    mid[s, 0] = m[0]
                    mid[s, 1] = m[1]
            if "c" in stages:
                if "b" not in stages:
                    m = (mid[s, 0], mid[s, 1])
                f = forward_two(m, tab)
                back = inverse_two(cjmul((prop[0], prop[1]), f), tab)
                add_window(grad, 0, r, c, cjmul((probe[0], probe[1]), back))

        return 0

    lax.fori_loop(0, SLOTS, step, 0)


def edges_of(grad, mid_l, mid_r, end_l, end_r):
    for mid, end, cols in ((mid_l, end_l, pl.ds(0, HALF)), (mid_r, end_r, pl.ds(COLS, HALF))):
        mid[...] = grad[:, HALF:ROWS, cols]
        end[:, :HALF, :] = grad[:, :HALF, cols]
        end[:, HALF:, :] = grad[:, ROWS:, cols]


def early_kernel(count, orow, ocol, wbatch, tab, probe, prop, state, between):
    windows(0, "a", count, orow, ocol, wbatch, tab, probe, prop, None, state, None, between, None)


def first_kernel(count, orow, ocol, wbatch, tab, probe, prop, amp, state, between, _, grad, *out):
    windows(0, "bc", count, orow, ocol, wbatch, tab, probe, prop, amp, state, grad, between, None)
    edges_of(grad, *out)


def batch_kernel(batch):
    def run(count, orow, ocol, wbatch, tab, probe, prop, amp, old, *rest):
        sides, (state, grad), out = rest[1:5], rest[5:7], rest[7:]
        fold_sides(old, state, *sides)
        windows(batch, "abc", count, orow, ocol, wbatch, tab, probe, prop, amp, state, grad, None, None)
        edges_of(grad, *out)

    return run


def final_kernel(count, orow, ocol, wbatch, tab, probe, prop, amp, old, *rest):
    sides, (state, grad, mid, side_r) = rest[1:5], rest[5:]
    fold_sides(old, state, *sides)
    windows(BATCHES - 1, "ab", count, orow, ocol, wbatch, tab, probe, prop, amp, state, grad, None, mid)
    side_r[...] = grad[2:, HALF:ROWS, COLS:]


def late_kernel(count, orow, ocol, wbatch, tab, probe, prop, mid, old, grad, side_r, corner, low):
    windows(BATCHES - 1, "c", count, orow, ocol, wbatch, tab, probe, prop, None, None, grad, None, mid)
    side_r[...] = grad[:2, HALF:ROWS, COLS:]
    corner[...] = grad[:, ROWS:, COLS:]
    low[...] = grad[:, ROWS:, :COLS]


def flat_kernel(grad, end_l, end_r, top, bottom):
    h = HALF
    for at, flat, ends in ((0, top, pl.ds(0, h)), (ROWS, bottom, pl.ds(h, h))):
        rows = pl.ds(at, h)
        flat[:, :, :h] = grad[:, rows, :h] + end_l[:, ends]
        flat[:, :, h:COLS] = grad[:, rows, h:COLS]
        flat[:, :, COLS:] = grad[:, rows, COLS:] + end_r[:, ends]


def settle_kernel(state, grad, end_l, end_r, out, blank):
    in_r = jnp.where(inside("row"), 0.5, 0.0).astype(f32)
    in_c = jnp.where(inside("col"), 1.0, 0.0).astype(f32)
    h = HALF
    for p in range(4):
        for at, ends in ((0, pl.ds(0, h)), (h, None), (ROWS, pl.ds(h, h))):
            rows = pl.ds(at, ROWS - h if ends is None else h)
            left, mid, right = grad[p, rows, :h], grad[p, rows, h:COLS], grad[p, rows, COLS:]
            if ends is not None:
                left = left + end_l[p, ends]
                right = right + end_r[p, ends]
            scale = in_r if at == ROWS else jnp.float32(0.5)
            out[p, rows, :h] = state[p, rows, :h] - scale * left
            out[p, rows, h:COLS] = state[p, rows, h:COLS] - scale * mid
            out[p, rows, COLS:] = state[p, rows, COLS:] - (scale * in_c) * right
            blank[p, rows, :] = jnp.zeros((left.shape[0], EXT_C), f32)


def final_settle_kernel(state, grad, corner, out, end_r):
    for p in range(4):
        end_r[p] = grad[p, :HALF, COLS:] + corner[p]
        out[p] = state[p, :ROWS, :COLS] - 0.5 * grad[p, :ROWS, :COLS]


def last_kernel(state, mid1, mid2, end, low, out):
    h = HALF
    for p in range(4):
        q = (p // 2, p % 2)
        mid = (mid1, mid2)[p // 2]
        out[(*q, slice(0, h), slice(0, h))] = state[p, :h, :h] - 0.5 * (end[p] + low[p, :, :h])
        out[(*q, slice(h, ROWS), slice(0, h))] = state[p, h:, :h] - 0.5 * mid[p % 2]
        out[(*q, slice(0, h), slice(h, COLS))] = state[p, :h, h:] - 0.5 * low[p, :, h:]
        out[(*q, slice(h, ROWS), slice(h, COLS))] = state[p, h:, h:]


VM = pl.BlockSpec(memory_space=pltpu.VMEM)
SM = pl.BlockSpec(memory_space=pltpu.SMEM)
EXT = (4, EXT_R, EXT_C)
EDGE = (4, HALF, 2 * HALF)
CORE = (4, HALF, HALF)
FLAT = (4, HALF, EXT_C)
SIDE = (2, ROWS - HALF, HALF)
PLANES = (SLOTS, 2, WIN, WIN)
MIDS = (4, ROWS - HALF, HALF)
ENDS = (4, 2 * HALF, HALF)


def call(kernel, scalars, arrays, outs, alias=None, limit=24):
    return pl.pallas_call(
        kernel,
        in_specs=[SM] * len(scalars) + [VM] * len(arrays),
        out_specs=[VM] * len(outs),
        out_shape=[jax.ShapeDtypeStruct(s, f32) for s in outs],
        input_output_aliases=alias or {},
        compiler_params=pltpu.CompilerParams(vmem_limit_bytes=limit * 2**20),
    )(*scalars, *arrays)


def from_behind(array, axis, by):
    size = lax.axis_size(axis)
    pairs = [(i, i + by) for i in range(size) if 0 <= i + by < size]
    return lax.ppermute(array, axis, pairs)


def body(transmission, probe, phase, amplitude, count, orow, ocol, wbatch):
    tab = jnp.asarray(dft_tables())
    scalars = (count, orow, ocol, wbatch)
    h = HALF
    planes = transmission.reshape(4, ROWS, COLS)
    right_top = from_behind(planes[:, :h, :h], "col", -1)
    right_1 = from_behind(planes[:2, h:, :h], "col", -1)
    right_2 = from_behind(planes[2:, h:, :h], "col", -1)
    amp, prop, grad = call(
        prep_kernel, (), (amplitude, phase), [(SLOTS, WIN, WIN), (2, WIN, WIN), EXT]
    )
    low = cc([planes[:, :h, :], right_top], 2)
    bottom = from_behind(low, "row", -1)
    (state,) = call(assemble_kernel, (), (transmission, right_top, right_1, bottom), [EXT])
    (between,) = call(early_kernel, scalars, (tab, probe, prop, state), [PLANES])
    (state,) = call(
        assemble_kernel, (), (transmission, right_top, right_2, bottom, state), [EXT], {4: 0}
    )
    edges = [MIDS, MIDS, ENDS, ENDS]
    for b in range(BATCHES - 1):
        common = (tab, probe, prop, amp, state)
        if b == 0:
            grad, *sent = call(
                first_kernel, scalars, (*common, between, grad), [EXT, *edges], {10: 0}
            )
        else:
            state, grad, *sent = call(
                batch_kernel(b), scalars, (*common, grad, *parts), [EXT, EXT, *edges], {8: 0, 9: 1}
            )
        mid_l, mid_r, end_l, end_r = sent
        from_left = from_behind(end_r, "col", 1)
        from_right = from_behind(end_l, "col", -1)
        mid_left = from_behind(mid_r, "col", 1)
        mid_right = from_behind(mid_l, "col", -1)
        top, bottom = call(flat_kernel, (), (grad, from_left, from_right), [FLAT, FLAT])
        above = from_behind(bottom, "row", 1)
        below = from_behind(top, "row", -1)
        state, grad = call(
            settle_kernel, (), (state, grad, from_left, from_right), [EXT, EXT], {0: 0, 1: 1}
        )
        parts = (mid_left, mid_right, above, below)
    state, grad, mid, side_2 = call(
        final_kernel,
        scalars,
        (tab, probe, prop, amp, state, grad, *parts),
        [EXT, EXT, PLANES, SIDE],
        {8: 0, 9: 1},
    )
    mid_2 = from_behind(side_2, "col", 1)
    grad, side_1, corner, low = call(
        late_kernel, scalars, (tab, probe, prop, mid, grad), [EXT, SIDE, CORE, EDGE], {8: 0}
    )
    mid_1 = from_behind(side_1, "col", 1)
    corner = from_behind(corner, "row", 1)
    low = from_behind(low, "row", 1)
    main, end_r = call(final_settle_kernel, (), (state, grad, corner), [(4, ROWS, COLS), CORE])
    end = from_behind(end_r, "col", 1)
    return call(last_kernel, (), (main, mid_1, mid_2, end, low), [(2, 2, ROWS, COLS)])[0]


def solution(mesh):
    in_specs = (
        P(None, None, "row", "col"),
        P(),
        P(),
        P("row", "col", None, None, None),
        P("row", "col"),
        P("row", "col", None),
        P("row", "col", None),
        P("row", "col", None),
    )
    out_specs = P(None, None, "row", "col")
    return jax.shard_map(body, mesh=mesh, in_specs=in_specs, out_specs=out_specs, check_vma=False)
```

```python
import math

import jax
import jax.numpy as jnp
import numpy as np
from jax import lax
from jax.experimental import pallas as pl
from jax.experimental.pallas import tpu as pltpu
from jax.sharding import PartitionSpec as P

BATCHES = 3
WIN = 256
HALF = 128
SLOTS = 4
ROWS = 512
COLS = 256
EXT_R = 640
EXT_C = 384


cc = jnp.concatenate
f32 = jnp.float32
bf16 = jnp.bfloat16


def dft_tables():
    n = np.arange(HALF)
    even = np.exp(-2j * np.pi * (np.outer(n, n) % HALF) / HALF) / math.sqrt(WIN)
    odd = np.exp(-2j * np.pi * n / WIN)[:, None] * even
    out = []
    for m in (even, odd):
        full = np.block([[m.real, m.imag], [-m.imag, m.real]]).astype(np.float32)
        for t in (full, full.T):
            hi = t.astype(bf16)
            lo = (t - hi.astype(np.float32)).astype(bf16)
            out.append(np.stack([hi, lo]))
    return np.stack(out).reshape(2, 2, 2, WIN, WIN)


def order_matrices():
    rows = lax.broadcasted_iota(jnp.int32, (WIN, WIN), 0)
    cols = lax.broadcasted_iota(jnp.int32, (WIN, WIN), 1)

    def source(k):
        return jnp.where(k < HALF, 2 * k, 2 * k - (WIN - 1))

    one, none = jnp.float32(1.0), jnp.float32(0.0)
    return [
        jnp.where(rows == source(cols), one, none).astype(bf16),
        jnp.where(cols == source(rows), one, none).astype(bf16),
    ]


def halves(x):
    hi = x.astype(bf16)
    lo = (x - hi.astype(f32)).astype(bf16)
    return hi, lo


PAIRED = [b for i in range(8) for b in (i, i + 8)]
NATURAL = [PAIRED.index(b) for b in range(16)]


def blocks(x, order):
    return cc([x[16 * b : 16 * b + 16] for b in order], 0)


def dot_r(x, tab, which, trans):
    hi, lo = halves(blocks(x, PAIRED))
    th = tab[which, trans, 0]
    t = cc([th, th, tab[which, trans, 1]], 0)
    return blocks(jnp.dot(cc([hi, lo, hi], 1), t, preferred_element_type=f32), NATURAL)


def dot_l(tab, which, trans, x):
    hi, lo = halves(x)
    th = tab[which, trans, 0]
    t = blocks(cc([th, th, tab[which, trans, 1]], 1), PAIRED)
    return blocks(jnp.dot(t, cc([hi, lo, hi], 0), preferred_element_type=f32), NATURAL)


def forward_two(z, tab):
    re, im = z
    h = HALF
    a = dot_r(cc([re[:, :h] + re[:, h:], im[:, :h] + im[:, h:]], 1), tab, 0, 0)
    b = dot_r(cc([re[:, :h] - re[:, h:], im[:, :h] - im[:, h:]], 1), tab, 1, 0)
    re, im = cc([a[:, :h], b[:, :h]], 1), cc([a[:, h:], b[:, h:]], 1)
    a = dot_l(tab, 0, 1, cc([re[:h] + re[h:], im[:h] + im[h:]], 0))
    b = dot_l(tab, 1, 1, cc([re[:h] - re[h:], im[:h] - im[h:]], 0))
    return cc([a[:h], b[:h]], 0), cc([a[h:], b[h:]], 0)


def inverse_two(z, tab):
    re, im = z
    h = HALF
    a = dot_l(tab, 0, 0, cc([re[:h], im[:h]], 0))
    b = dot_l(tab, 1, 0, cc([re[h:], im[h:]], 0))
    s, d = a + b, a - b
    re, im = cc([s[:h], d[:h]], 0), cc([s[h:], d[h:]], 0)
    a = dot_r(cc([re[:, :h], im[:, :h]], 1), tab, 0, 1)
    b = dot_r(cc([re[:, h:], im[:, h:]], 1), tab, 1, 1)
    s, d = a + b, a - b
    return cc([s[:, :h], d[:, :h]], 1), cc([s[:, h:], d[:, h:]], 1)


def cmul(a, b):
    return a[0] * b[0] - a[1] * b[1], a[0] * b[1] + a[1] * b[0]


def cjmul(a, b):
    return a[0] * b[0] + a[1] * b[1], a[0] * b[1] - a[1] * b[0]


def place(r):
    base = pl.multiple_of(jnp.minimum(r // 8 * 8, EXT_R - WIN - 8), 8)
    return base, r - base


def lanes_left(x, c):
    keep = lax.broadcasted_iota(jnp.int32, (x.shape[0], HALF), 1) < HALF - c
    turn = lax.rem(HALF - c, HALF)
    a, b, d = [pltpu.roll(x[:, i * HALF : (i + 1) * HALF], turn, 1) for i in range(3)]
    return cc([jnp.where(keep, a, b), jnp.where(keep, b, d)], 1)


def lanes_right(x, c):
    keep = lax.broadcasted_iota(jnp.int32, (x.shape[0], HALF), 1) >= c
    turn = lax.rem(c, HALF)
    a, b = [pltpu.roll(x[:, i * HALF : (i + 1) * HALF], turn, 1) for i in range(2)]
    none = jnp.zeros_like(a)
    return cc([jnp.where(keep, a, none), jnp.where(keep, b, a), jnp.where(keep, none, b)], 1)


def rows_up(x, shift):
    y = x.reshape(WIN // 8 + 1, 8, x.shape[1])
    y = pltpu.roll(y, lax.rem(8 - shift, 8), 1)
    keep = lax.broadcasted_iota(jnp.int32, (WIN // 8, 8, x.shape[1]), 1) < 8 - shift
    return jnp.where(keep, y[:-1], y[1:]).reshape(WIN, x.shape[1])


def rows_down(x, shift):
    y = x.reshape(WIN // 8, 8, x.shape[1])
    y = pltpu.roll(y, lax.rem(shift, 8), 1)
    none = jnp.zeros((1, 8, x.shape[1]), f32)
    keep = lax.broadcasted_iota(jnp.int32, (WIN // 8 + 1, 8, x.shape[1]), 1) >= shift
    return jnp.where(keep, cc([y, none], 0), cc([none, y], 0)).reshape(WIN + 8, x.shape[1])


def load_window(ref, first, r, c):
    base, shift = place(r)
    out = []
    for p in (first, first + 1):
        t = lanes_left(ref[p, pl.ds(base, WIN + 8), :], c)
        out.append(rows_up(t, shift))
    return out


def add_window(ref, first, r, c, g):
    base, shift = place(r)
    for p in (first, first + 1):
        t = lanes_right(rows_down(g[p - first], shift), c)
        ref[p, pl.ds(base, WIN + 8), :] = ref[p, pl.ds(base, WIN + 8), :] + t


def reorder(x, order):
    a = x.astype(bf16)
    rest = x - a.astype(f32)
    b = rest.astype(bf16)
    c = (rest - b.astype(f32)).astype(bf16)
    m = order[0]
    y = jnp.dot(a, m, preferred_element_type=f32)
    y = y + jnp.dot(b, m, preferred_element_type=f32)
    y = y + jnp.dot(c, m, preferred_element_type=f32)
    a = y.astype(bf16)
    rest = y - a.astype(f32)
    b = rest.astype(bf16)
    c = (rest - b.astype(f32)).astype(bf16)
    m = order[1]
    y = jnp.dot(m, a, preferred_element_type=f32)
    y = y + jnp.dot(m, b, preferred_element_type=f32)
    return y + jnp.dot(m, c, preferred_element_type=f32)


def prep_kernel(amp, phase, amp_out, prop_out, grad):
    grad[...] = jnp.zeros_like(grad)
    order = order_matrices()

    def step(s, _):
        amp_out[s] = reorder(amp[0, 0, s], order)
        return 0

    lax.fori_loop(0, SLOTS, step, 0)
    ph = reorder(phase[...], order)
    prop_out[0] = jnp.cos(ph)
    prop_out[1] = jnp.sin(ph)


def inside(axis):
    return lax.axis_index(axis) < lax.axis_size(axis) - 1


def assemble_kernel(main, right_top, right_rest, bottom, *rest):
    state = rest[-1]
    first = 0 if len(rest) == 1 else 2
    for k in range(2):
        p = first + k
        state[p, :ROWS, :COLS] = main[first // 2, k]
        state[p, :HALF, COLS:] = right_top[p]
        state[p, HALF:ROWS, COLS:] = right_rest[k]
        state[p, ROWS:, :] = bottom[p]


def fold_sides(old, state, mid_l, mid_r, above, below, core_a, core_b):
    in_c = jnp.where(inside("col"), 1.0, 0.0).astype(f32)
    in_r = jnp.where(inside("row"), 1.0, 0.0).astype(f32)
    rows = pl.ds(HALF, ROWS - HALF)
    for p in range(4):
        state[p, rows, :HALF] = old[p, rows, :HALF] - 0.5 * mid_l[p]
        state[p, rows, COLS:] = old[p, rows, COLS:] - (0.5 * in_c) * mid_r[p]
        for at, fac, near, core in (
            (pl.ds(0, HALF), 0.5, above, core_a),
            (pl.ds(ROWS, HALF), 0.5 * in_r, below, core_b),
        ):
            state[p, at, :HALF] = old[p, at, :HALF] - fac * near[p, :, :HALF]
            state[p, at, HALF:COLS] = old[p, at, HALF:COLS] - fac * core[p]
            state[p, at, COLS:] = old[p, at, COLS:] - (fac * in_c) * near[p, :, HALF:]


def windows(batch, stages, count, orow, ocol, wbatch, tab, probe, prop, amp, state, grad, between, mid):
    def step(s, _):
        @pl.when((s < count[0, 0]) & (wbatch[0, 0, s] == batch))
        def _():
            r = orow[0, 0, s]
            c = ocol[0, 0, s]
            if "a" in stages:
                psi = cmul((probe[0], probe[1]), load_window(state, 0, r, c))
                f = forward_two(psi, tab)
                bt = inverse_two(cmul((prop[0], prop[1]), f), tab)
                if "b" not in stages:
                    between[s, 0] = bt[0]
                    between[s, 1] = bt[1]
            if "b" in stages:
                if "a" not in stages:
                    bt = (between[s, 0], between[s, 1])
                w2 = load_window(state, 2, r, c)
                far = forward_two(cmul(bt, w2), tab)
                power = far[0] * far[0] + far[1] * far[1]
                factor = 1.0 - amp[s] * lax.rsqrt(jnp.maximum(power, 1.0))
                back = inverse_two((far[0] * factor, far[1] * factor), tab)
                add_window(grad, 2, r, c, cjmul(bt, back))
                m = cjmul(w2, back)
                if "c" not in stages:
                    mid[s, 0] = m[0]
                    mid[s, 1] = m[1]
            if "c" in stages:
                if "b" not in stages:
                    m = (mid[s, 0], mid[s, 1])
                f = forward_two(m, tab)
                back = inverse_two(cjmul((prop[0], prop[1]), f), tab)
                add_window(grad, 0, r, c, cjmul((probe[0], probe[1]), back))

        return 0

    lax.fori_loop(0, SLOTS, step, 0)


def edges_of(grad, mid_l, mid_r, end_l, end_r, top_core, bottom_core):
    top_core[...] = grad[:, :HALF, HALF:COLS]
    bottom_core[...] = grad[:, ROWS:, HALF:COLS]
    for mid, end, cols in ((mid_l, end_l, pl.ds(0, HALF)), (mid_r, end_r, pl.ds(COLS, HALF))):
        mid[...] = grad[:, HALF:ROWS, cols]
        end[:, :HALF, :] = grad[:, :HALF, cols]
        end[:, HALF:, :] = grad[:, ROWS:, cols]


def early_kernel(count, orow, ocol, wbatch, tab, probe, prop, state, between):
    windows(0, "a", count, orow, ocol, wbatch, tab, probe, prop, None, state, None, between, None)


def first_kernel(count, orow, ocol, wbatch, tab, probe, prop, amp, state, between, _, grad, *out):
    windows(0, "bc", count, orow, ocol, wbatch, tab, probe, prop, amp, state, grad, between, None)
    edges_of(grad, *out)


def batch_kernel(batch):
    def run(count, orow, ocol, wbatch, tab, probe, prop, amp, old, *rest):
        sides, (state, grad), out = rest[1:7], rest[7:9], rest[9:]
        fold_sides(old, state, *sides)
        windows(batch, "abc", count, orow, ocol, wbatch, tab, probe, prop, amp, state, grad, None, None)
        edges_of(grad, *out)

    return run


def final_kernel(count, orow, ocol, wbatch, tab, probe, prop, amp, old, *rest):
    sides, (state, grad, mid, side_r) = rest[1:7], rest[7:]
    fold_sides(old, state, *sides)
    windows(BATCHES - 1, "ab", count, orow, ocol, wbatch, tab, probe, prop, amp, state, grad, None, mid)
    side_r[...] = grad[2:, HALF:ROWS, COLS:]


def late_kernel(count, orow, ocol, wbatch, tab, probe, prop, mid, old, grad, side_r, corner, low):
    windows(BATCHES - 1, "c", count, orow, ocol, wbatch, tab, probe, prop, None, None, grad, None, mid)
    side_r[...] = grad[:2, HALF:ROWS, COLS:]
    corner[...] = grad[:, ROWS:, COLS:]
    low[...] = grad[:, ROWS:, :COLS]


def flat_kernel(grad, end_l, end_r, top, bottom):
    h = HALF
    for at, flat, ends in ((0, top, pl.ds(0, h)), (ROWS, bottom, pl.ds(h, h))):
        rows = pl.ds(at, h)
        flat[:, :, :h] = grad[:, rows, :h] + end_l[:, ends]
        flat[:, :, h:] = grad[:, rows, COLS:] + end_r[:, ends]


def settle_kernel(state, grad, end_l, end_r, out, blank):
    in_r = jnp.where(inside("row"), 0.5, 0.0).astype(f32)
    in_c = jnp.where(inside("col"), 1.0, 0.0).astype(f32)
    h = HALF
    for p in range(4):
        for at, ends in ((0, pl.ds(0, h)), (h, None), (ROWS, pl.ds(h, h))):
            rows = pl.ds(at, ROWS - h if ends is None else h)
            left, mid, right = grad[p, rows, :h], grad[p, rows, h:COLS], grad[p, rows, COLS:]
            if ends is not None:
                left = left + end_l[p, ends]
                right = right + end_r[p, ends]
            scale = in_r if at == ROWS else jnp.float32(0.5)
            out[p, rows, :h] = state[p, rows, :h] - scale * left
            out[p, rows, h:COLS] = state[p, rows, h:COLS] - scale * mid
            out[p, rows, COLS:] = state[p, rows, COLS:] - (scale * in_c) * right
            blank[p, rows, :] = jnp.zeros((left.shape[0], EXT_C), f32)


def final_settle_kernel(state, grad, corner, out, end_r):
    for p in range(4):
        end_r[p] = grad[p, :HALF, COLS:] + corner[p]
        out[p] = state[p, :ROWS, :COLS] - 0.5 * grad[p, :ROWS, :COLS]


def last_kernel(state, mid1, mid2, end, low, out):
    h = HALF
    for p in range(4):
        q = (p // 2, p % 2)
        mid = (mid1, mid2)[p // 2]
        out[(*q, slice(0, h), slice(0, h))] = state[p, :h, :h] - 0.5 * (end[p] + low[p, :, :h])
        out[(*q, slice(h, ROWS), slice(0, h))] = state[p, h:, :h] - 0.5 * mid[p % 2]
        out[(*q, slice(0, h), slice(h, COLS))] = state[p, :h, h:] - 0.5 * low[p, :, h:]
        out[(*q, slice(h, ROWS), slice(h, COLS))] = state[p, h:, h:]


VM = pl.BlockSpec(memory_space=pltpu.VMEM)
SM = pl.BlockSpec(memory_space=pltpu.SMEM)
EXT = (4, EXT_R, EXT_C)
EDGE = (4, HALF, 2 * HALF)
CORE = (4, HALF, HALF)
SIDE = (2, ROWS - HALF, HALF)
PLANES = (SLOTS, 2, WIN, WIN)
MIDS = (4, ROWS - HALF, HALF)
ENDS = (4, 2 * HALF, HALF)


def call(kernel, scalars, arrays, outs, alias=None, limit=24):
    return pl.pallas_call(
        kernel,
        in_specs=[SM] * len(scalars) + [VM] * len(arrays),
        out_specs=[VM] * len(outs),
        out_shape=[jax.ShapeDtypeStruct(s, f32) for s in outs],
        input_output_aliases=alias or {},
        compiler_params=pltpu.CompilerParams(vmem_limit_bytes=limit * 2**20),
    )(*scalars, *arrays)


def from_behind(array, axis, by):
    size = lax.axis_size(axis)
    pairs = [(i, i + by) for i in range(size) if 0 <= i + by < size]
    return lax.ppermute(array, axis, pairs)


def body(transmission, probe, phase, amplitude, count, orow, ocol, wbatch):
    tab = jnp.asarray(dft_tables())
    scalars = (count, orow, ocol, wbatch)
    h = HALF
    planes = transmission.reshape(4, ROWS, COLS)
    right_top = from_behind(planes[:, :h, :h], "col", -1)
    right_1 = from_behind(planes[:2, h:, :h], "col", -1)
    right_2 = from_behind(planes[2:, h:, :h], "col", -1)
    amp, prop, grad = call(
        prep_kernel, (), (amplitude, phase), [(SLOTS, WIN, WIN), (2, WIN, WIN), EXT]
    )
    low = cc([planes[:, :h, :], right_top], 2)
    bottom = from_behind(low, "row", -1)
    (state,) = call(assemble_kernel, (), (transmission, right_top, right_1, bottom), [EXT])
    (between,) = call(early_kernel, scalars, (tab, probe, prop, state), [PLANES])
    (state,) = call(
        assemble_kernel, (), (transmission, right_top, right_2, bottom, state), [EXT], {4: 0}
    )
    edges = [MIDS, MIDS, ENDS, ENDS, CORE, CORE]
    for b in range(BATCHES - 1):
        common = (tab, probe, prop, amp, state)
        if b == 0:
            grad, *sent = call(
                first_kernel, scalars, (*common, between, grad), [EXT, *edges], {10: 0}
            )
        else:
            state, grad, *sent = call(
                batch_kernel(b), scalars, (*common, grad, *parts), [EXT, EXT, *edges], {8: 0, 9: 1}
            )
        mid_l, mid_r, end_l, end_r, top_core, bottom_core = sent
        from_left = from_behind(end_r, "col", 1)
        from_right = from_behind(end_l, "col", -1)
        mid_left = from_behind(mid_r, "col", 1)
        mid_right = from_behind(mid_l, "col", -1)
        core_a = from_behind(bottom_core, "row", 1)
        core_b = from_behind(top_core, "row", -1)
        top, bottom = call(flat_kernel, (), (grad, from_left, from_right), [EDGE, EDGE])
        above = from_behind(bottom, "row", 1)
        below = from_behind(top, "row", -1)
        state, grad = call(
            settle_kernel, (), (state, grad, from_left, from_right), [EXT, EXT], {0: 0, 1: 1}
        )
        parts = (mid_left, mid_right, above, below, core_a, core_b)
    state, grad, mid, side_2 = call(
        final_kernel,
        scalars,
        (tab, probe, prop, amp, state, grad, *parts),
        [EXT, EXT, PLANES, SIDE],
        {8: 0, 9: 1},
    )
    mid_2 = from_behind(side_2, "col", 1)
    grad, side_1, corner, low = call(
        late_kernel, scalars, (tab, probe, prop, mid, grad), [EXT, SIDE, CORE, EDGE], {8: 0}
    )
    mid_1 = from_behind(side_1, "col", 1)
    corner = from_behind(corner, "row", 1)
    low = from_behind(low, "row", 1)
    main, end_r = call(final_settle_kernel, (), (state, grad, corner), [(4, ROWS, COLS), CORE])
    end = from_behind(end_r, "col", 1)
    return call(last_kernel, (), (main, mid_1, mid_2, end, low), [(2, 2, ROWS, COLS)])[0]


def solution(mesh):
    in_specs = (
        P(None, None, "row", "col"),
        P(),
        P(),
        P("row", "col", None, None, None),
        P("row", "col"),
        P("row", "col", None),
        P("row", "col", None),
        P("row", "col", None),
    )
    out_specs = P(None, None, "row", "col")
    return jax.shard_map(body, mesh=mesh, in_specs=in_specs, out_specs=out_specs, check_vma=False)
```

```python
import math

import jax
import jax.numpy as jnp
import numpy as np
from jax import lax
from jax.experimental import pallas as pl
from jax.experimental.pallas import tpu as pltpu
from jax.sharding import PartitionSpec as P

BATCHES = 3
WIN = 256
HALF = 128
SLOTS = 4
ROWS = 512
COLS = 256
EXT_R = 640
EXT_C = 384


cc = jnp.concatenate
f32 = jnp.float32
bf16 = jnp.bfloat16


def dft_tables():
    n = np.arange(HALF)
    even = np.exp(-2j * np.pi * (np.outer(n, n) % HALF) / HALF) / math.sqrt(WIN)
    odd = np.exp(-2j * np.pi * n / WIN)[:, None] * even
    out = []
    for m in (even, odd):
        full = np.block([[m.real, m.imag], [-m.imag, m.real]]).astype(np.float32)
        for t in (full, full.T):
            hi = t.astype(bf16)
            lo = (t - hi.astype(np.float32)).astype(bf16)
            out.append(np.stack([hi, lo]))
    return np.stack(out).reshape(2, 2, 2, WIN, WIN)


def order_matrices():
    rows = lax.broadcasted_iota(jnp.int32, (WIN, WIN), 0)
    cols = lax.broadcasted_iota(jnp.int32, (WIN, WIN), 1)

    def source(k):
        return jnp.where(k < HALF, 2 * k, 2 * k - (WIN - 1))

    one, none = jnp.float32(1.0), jnp.float32(0.0)
    return [
        jnp.where(rows == source(cols), one, none).astype(bf16),
        jnp.where(cols == source(rows), one, none).astype(bf16),
    ]


def halves(x):
    hi = x.astype(bf16)
    lo = (x - hi.astype(f32)).astype(bf16)
    return hi, lo


PAIRED = [b for i in range(8) for b in (i, i + 8)]
NATURAL = [PAIRED.index(b) for b in range(16)]


def blocks(x, order):
    return cc([x[16 * b : 16 * b + 16] for b in order], 0)


def dot_r(x, tab, which, trans):
    hi, lo = halves(blocks(x, PAIRED))
    th = tab[which, trans, 0]
    t = cc([th, th, tab[which, trans, 1]], 0)
    return blocks(jnp.dot(cc([hi, lo, hi], 1), t, preferred_element_type=f32), NATURAL)


def dot_l(tab, which, trans, x):
    hi, lo = halves(x)
    th = tab[which, trans, 0]
    t = blocks(cc([th, th, tab[which, trans, 1]], 1), PAIRED)
    return blocks(jnp.dot(t, cc([hi, lo, hi], 0), preferred_element_type=f32), NATURAL)


def forward_two(z, tab):
    re, im = z
    h = HALF
    a = dot_r(cc([re[:, :h] + re[:, h:], im[:, :h] + im[:, h:]], 1), tab, 0, 0)
    b = dot_r(cc([re[:, :h] - re[:, h:], im[:, :h] - im[:, h:]], 1), tab, 1, 0)
    re, im = cc([a[:, :h], b[:, :h]], 1), cc([a[:, h:], b[:, h:]], 1)
    a = dot_l(tab, 0, 1, cc([re[:h] + re[h:], im[:h] + im[h:]], 0))
    b = dot_l(tab, 1, 1, cc([re[:h] - re[h:], im[:h] - im[h:]], 0))
    return cc([a[:h], b[:h]], 0), cc([a[h:], b[h:]], 0)


def inverse_two(z, tab):
    re, im = z
    h = HALF
    a = dot_l(tab, 0, 0, cc([re[:h], im[:h]], 0))
    b = dot_l(tab, 1, 0, cc([re[h:], im[h:]], 0))
    s, d = a + b, a - b
    re, im = cc([s[:h], d[:h]], 0), cc([s[h:], d[h:]], 0)
    a = dot_r(cc([re[:, :h], im[:, :h]], 1), tab, 0, 1)
    b = dot_r(cc([re[:, h:], im[:, h:]], 1), tab, 1, 1)
    s, d = a + b, a - b
    return cc([s[:, :h], d[:, :h]], 1), cc([s[:, h:], d[:, h:]], 1)


def cmul(a, b):
    return a[0] * b[0] - a[1] * b[1], a[0] * b[1] + a[1] * b[0]


def cjmul(a, b):
    return a[0] * b[0] + a[1] * b[1], a[0] * b[1] - a[1] * b[0]


def place(r):
    base = pl.multiple_of(jnp.minimum(r // 8 * 8, EXT_R - WIN - 8), 8)
    return base, r - base


def lanes_left(x, c):
    keep = lax.broadcasted_iota(jnp.int32, (x.shape[0], HALF), 1) < HALF - c
    turn = lax.rem(HALF - c, HALF)
    a, b, d = [pltpu.roll(x[:, i * HALF : (i + 1) * HALF], turn, 1) for i in range(3)]
    return cc([jnp.where(keep, a, b), jnp.where(keep, b, d)], 1)


def lanes_right(x, c):
    keep = lax.broadcasted_iota(jnp.int32, (x.shape[0], HALF), 1) >= c
    turn = lax.rem(c, HALF)
    a, b = [pltpu.roll(x[:, i * HALF : (i + 1) * HALF], turn, 1) for i in range(2)]
    none = jnp.zeros_like(a)
    return cc([jnp.where(keep, a, none), jnp.where(keep, b, a), jnp.where(keep, none, b)], 1)


def rows_up(x, shift):
    y = x.reshape(WIN // 8 + 1, 8, x.shape[1])
    y = pltpu.roll(y, lax.rem(8 - shift, 8), 1)
    keep = lax.broadcasted_iota(jnp.int32, (WIN // 8, 8, x.shape[1]), 1) < 8 - shift
    return jnp.where(keep, y[:-1], y[1:]).reshape(WIN, x.shape[1])


def rows_down(x, shift):
    y = x.reshape(WIN // 8, 8, x.shape[1])
    y = pltpu.roll(y, lax.rem(shift, 8), 1)
    none = jnp.zeros((1, 8, x.shape[1]), f32)
    keep = lax.broadcasted_iota(jnp.int32, (WIN // 8 + 1, 8, x.shape[1]), 1) >= shift
    return jnp.where(keep, cc([y, none], 0), cc([none, y], 0)).reshape(WIN + 8, x.shape[1])


def load_window(ref, first, r, c):
    base, shift = place(r)
    out = []
    for p in (first, first + 1):
        t = lanes_left(ref[p, pl.ds(base, WIN + 8), :], c)
        out.append(rows_up(t, shift))
    return out


def add_window(ref, first, r, c, g):
    base, shift = place(r)
    for p in (first, first + 1):
        t = lanes_right(rows_down(g[p - first], shift), c)
        ref[p, pl.ds(base, WIN + 8), :] = ref[p, pl.ds(base, WIN + 8), :] + t


def reorder(x, order):
    a = x.astype(bf16)
    rest = x - a.astype(f32)
    b = rest.astype(bf16)
    c = (rest - b.astype(f32)).astype(bf16)
    m = order[0]
    y = jnp.dot(a, m, preferred_element_type=f32)
    y = y + jnp.dot(b, m, preferred_element_type=f32)
    y = y + jnp.dot(c, m, preferred_element_type=f32)
    a = y.astype(bf16)
    rest = y - a.astype(f32)
    b = rest.astype(bf16)
    c = (rest - b.astype(f32)).astype(bf16)
    m = order[1]
    y = jnp.dot(m, a, preferred_element_type=f32)
    y = y + jnp.dot(m, b, preferred_element_type=f32)
    return y + jnp.dot(m, c, preferred_element_type=f32)


def prep_kernel(amp, phase, amp_out, prop_out, grad):
    grad[...] = jnp.zeros_like(grad)
    order = order_matrices()

    def step(s, _):
        amp_out[s] = reorder(amp[0, 0, s], order)
        return 0

    lax.fori_loop(0, SLOTS, step, 0)
    ph = reorder(phase[...], order)
    prop_out[0] = jnp.cos(ph)
    prop_out[1] = jnp.sin(ph)


def inside(axis):
    return lax.axis_index(axis) < lax.axis_size(axis) - 1


def assemble_kernel(main, right_top, right_rest, bottom, corner, *rest):
    state = rest[-1]
    first = 0 if len(rest) == 1 else 2
    for k in range(2):
        p = first + k
        state[p, :ROWS, :COLS] = main[first // 2, k]
        state[p, :HALF, COLS:] = right_top[p]
        state[p, HALF:ROWS, COLS:] = right_rest[k]
        state[p, ROWS:, :COLS] = bottom[p]
        state[p, ROWS:, COLS:] = corner[p]


def fold_sides(old, state, mid_l, mid_r, above, below, core_a, core_b):
    in_c = jnp.where(inside("col"), 1.0, 0.0).astype(f32)
    in_r = jnp.where(inside("row"), 1.0, 0.0).astype(f32)
    rows = pl.ds(HALF, ROWS - HALF)
    for p in range(4):
        state[p, rows, :HALF] = old[p, rows, :HALF] - 0.5 * mid_l[p]
        state[p, rows, COLS:] = old[p, rows, COLS:] - (0.5 * in_c) * mid_r[p]
        for at, fac, near, core in (
            (pl.ds(0, HALF), 0.5, above, core_a),
            (pl.ds(ROWS, HALF), 0.5 * in_r, below, core_b),
        ):
            state[p, at, :HALF] = old[p, at, :HALF] - fac * near[p, :, :HALF]
            state[p, at, HALF:COLS] = old[p, at, HALF:COLS] - fac * core[p]
            state[p, at, COLS:] = old[p, at, COLS:] - (fac * in_c) * near[p, :, HALF:]


def windows(batch, stages, count, orow, ocol, wbatch, tab, probe, prop, amp, state, grad, between, mid):
    def step(s, _):
        @pl.when((s < count[0, 0]) & (wbatch[0, 0, s] == batch))
        def _():
            r = orow[0, 0, s]
            c = ocol[0, 0, s]
            if "a" in stages:
                psi = cmul((probe[0], probe[1]), load_window(state, 0, r, c))
                f = forward_two(psi, tab)
                bt = inverse_two(cmul((prop[0], prop[1]), f), tab)
                if "b" not in stages:
                    between[s, 0] = bt[0]
                    between[s, 1] = bt[1]
            if "b" in stages:
                if "a" not in stages:
                    bt = (between[s, 0], between[s, 1])
                w2 = load_window(state, 2, r, c)
                far = forward_two(cmul(bt, w2), tab)
                power = far[0] * far[0] + far[1] * far[1]
                factor = 1.0 - amp[s] * lax.rsqrt(jnp.maximum(power, 1.0))
                back = inverse_two((far[0] * factor, far[1] * factor), tab)
                add_window(grad, 2, r, c, cjmul(bt, back))
                m = cjmul(w2, back)
                if "c" not in stages:
                    mid[s, 0] = m[0]
                    mid[s, 1] = m[1]
            if "c" in stages:
                if "b" not in stages:
                    m = (mid[s, 0], mid[s, 1])
                f = forward_two(m, tab)
                back = inverse_two(cjmul((prop[0], prop[1]), f), tab)
                add_window(grad, 0, r, c, cjmul((probe[0], probe[1]), back))

        return 0

    lax.fori_loop(0, SLOTS, step, 0)


def edges_of(grad, mid_l, mid_r, end_l, end_r, top_core, bottom_core):
    top_core[...] = grad[:, :HALF, HALF:COLS]
    bottom_core[...] = grad[:, ROWS:, HALF:COLS]
    for mid, end, cols in ((mid_l, end_l, pl.ds(0, HALF)), (mid_r, end_r, pl.ds(COLS, HALF))):
        mid[...] = grad[:, HALF:ROWS, cols]
        end[:, :HALF, :] = grad[:, :HALF, cols]
        end[:, HALF:, :] = grad[:, ROWS:, cols]


def early_kernel(count, orow, ocol, wbatch, tab, probe, prop, state, between):
    windows(0, "a", count, orow, ocol, wbatch, tab, probe, prop, None, state, None, between, None)


def first_kernel(count, orow, ocol, wbatch, tab, probe, prop, amp, state, between, _, grad, *out):
    windows(0, "bc", count, orow, ocol, wbatch, tab, probe, prop, amp, state, grad, between, None)
    edges_of(grad, *out)


def batch_kernel(batch):
    def run(count, orow, ocol, wbatch, tab, probe, prop, amp, old, *rest):
        sides, (state, grad), out = rest[1:7], rest[7:9], rest[9:]
        fold_sides(old, state, *sides)
        windows(batch, "abc", count, orow, ocol, wbatch, tab, probe, prop, amp, state, grad, None, None)
        edges_of(grad, *out)

    return run


def final_kernel(count, orow, ocol, wbatch, tab, probe, prop, amp, old, *rest):
    sides, (state, grad, mid, side_r) = rest[1:7], rest[7:]
    fold_sides(old, state, *sides)
    windows(BATCHES - 1, "ab", count, orow, ocol, wbatch, tab, probe, prop, amp, state, grad, None, mid)
    side_r[...] = grad[2:, HALF:ROWS, COLS:]


def late_kernel(count, orow, ocol, wbatch, tab, probe, prop, mid, old, grad, side_r, corner, low):
    windows(BATCHES - 1, "c", count, orow, ocol, wbatch, tab, probe, prop, None, None, grad, None, mid)
    side_r[...] = grad[:2, HALF:ROWS, COLS:]
    corner[...] = grad[:, ROWS:, COLS:]
    low[...] = grad[:, ROWS:, :COLS]


def flat_kernel(grad, end_l, end_r, top, bottom):
    h = HALF
    for at, flat, ends in ((0, top, pl.ds(0, h)), (ROWS, bottom, pl.ds(h, h))):
        rows = pl.ds(at, h)
        flat[:, :, :h] = grad[:, rows, :h] + end_l[:, ends]
        flat[:, :, h:] = grad[:, rows, COLS:] + end_r[:, ends]


def settle_kernel(state, grad, end_l, end_r, out, blank):
    in_r = jnp.where(inside("row"), 0.5, 0.0).astype(f32)
    in_c = jnp.where(inside("col"), 1.0, 0.0).astype(f32)
    h = HALF
    for p in range(4):
        for at, ends in ((0, pl.ds(0, h)), (h, None), (ROWS, pl.ds(h, h))):
            rows = pl.ds(at, ROWS - h if ends is None else h)
            left, mid, right = grad[p, rows, :h], grad[p, rows, h:COLS], grad[p, rows, COLS:]
            if ends is not None:
                left = left + end_l[p, ends]
                right = right + end_r[p, ends]
            scale = in_r if at == ROWS else jnp.float32(0.5)
            out[p, rows, :h] = state[p, rows, :h] - scale * left
            out[p, rows, h:COLS] = state[p, rows, h:COLS] - scale * mid
            out[p, rows, COLS:] = state[p, rows, COLS:] - (scale * in_c) * right
            blank[p, rows, :] = jnp.zeros((left.shape[0], EXT_C), f32)


def final_settle_kernel(state, grad, corner, out, end_r):
    for p in range(4):
        end_r[p] = grad[p, :HALF, COLS:] + corner[p]
        out[p] = state[p, :ROWS, :COLS] - 0.5 * grad[p, :ROWS, :COLS]


def last_kernel(state, mid1, mid2, end, low, out):
    h = HALF
    for p in range(4):
        q = (p // 2, p % 2)
        mid = (mid1, mid2)[p // 2]
        out[(*q, slice(0, h), slice(0, h))] = state[p, :h, :h] - 0.5 * (end[p] + low[p, :, :h])
        out[(*q, slice(h, ROWS), slice(0, h))] = state[p, h:, :h] - 0.5 * mid[p % 2]
        out[(*q, slice(0, h), slice(h, COLS))] = state[p, :h, h:] - 0.5 * low[p, :, h:]
        out[(*q, slice(h, ROWS), slice(h, COLS))] = state[p, h:, h:]


VM = pl.BlockSpec(memory_space=pltpu.VMEM)
SM = pl.BlockSpec(memory_space=pltpu.SMEM)
EXT = (4, EXT_R, EXT_C)
EDGE = (4, HALF, 2 * HALF)
CORE = (4, HALF, HALF)
SIDE = (2, ROWS - HALF, HALF)
PLANES = (SLOTS, 2, WIN, WIN)
MIDS = (4, ROWS - HALF, HALF)
ENDS = (4, 2 * HALF, HALF)


def call(kernel, scalars, arrays, outs, alias=None, limit=24):
    return pl.pallas_call(
        kernel,
        in_specs=[SM] * len(scalars) + [VM] * len(arrays),
        out_specs=[VM] * len(outs),
        out_shape=[jax.ShapeDtypeStruct(s, f32) for s in outs],
        input_output_aliases=alias or {},
        compiler_params=pltpu.CompilerParams(vmem_limit_bytes=limit * 2**20),
    )(*scalars, *arrays)


def from_behind(array, axis, by):
    size = lax.axis_size(axis)
    pairs = [(i, i + by) for i in range(size) if 0 <= i + by < size]
    return lax.ppermute(array, axis, pairs)


def body(transmission, probe, phase, amplitude, count, orow, ocol, wbatch):
    tab = jnp.asarray(dft_tables())
    scalars = (count, orow, ocol, wbatch)
    h = HALF
    planes = transmission.reshape(4, ROWS, COLS)
    right_top = from_behind(planes[:, :h, :h], "col", -1)
    right_1 = from_behind(planes[:2, h:, :h], "col", -1)
    right_2 = from_behind(planes[2:, h:, :h], "col", -1)
    amp, prop, grad = call(
        prep_kernel, (), (amplitude, phase), [(SLOTS, WIN, WIN), (2, WIN, WIN), EXT]
    )
    bottom = from_behind(planes[:, :h, :], "row", -1)
    corner = from_behind(right_top, "row", -1)
    (state,) = call(assemble_kernel, (), (transmission, right_top, right_1, bottom, corner), [EXT])
    (between,) = call(early_kernel, scalars, (tab, probe, prop, state), [PLANES])
    (state,) = call(
        assemble_kernel,
        (),
        (transmission, right_top, right_2, bottom, corner, state),
        [EXT],
        {5: 0},
    )
    edges = [MIDS, MIDS, ENDS, ENDS, CORE, CORE]
    for b in range(BATCHES - 1):
        common = (tab, probe, prop, amp, state)
        if b == 0:
            grad, *sent = call(
                first_kernel, scalars, (*common, between, grad), [EXT, *edges], {10: 0}
            )
        else:
            state, grad, *sent = call(
                batch_kernel(b), scalars, (*common, grad, *parts), [EXT, EXT, *edges], {8: 0, 9: 1}
            )
        mid_l, mid_r, end_l, end_r, top_core, bottom_core = sent
        from_left = from_behind(end_r, "col", 1)
        from_right = from_behind(end_l, "col", -1)
        mid_left = from_behind(mid_r, "col", 1)
        mid_right = from_behind(mid_l, "col", -1)
        core_a = from_behind(bottom_core, "row", 1)
        core_b = from_behind(top_core, "row", -1)
        top, bottom = call(flat_kernel, (), (grad, from_left, from_right), [EDGE, EDGE])
        above = from_behind(bottom, "row", 1)
        below = from_behind(top, "row", -1)
        state, grad = call(
            settle_kernel, (), (state, grad, from_left, from_right), [EXT, EXT], {0: 0, 1: 1}
        )
        parts = (mid_left, mid_right, above, below, core_a, core_b)
    state, grad, mid, side_2 = call(
        final_kernel,
        scalars,
        (tab, probe, prop, amp, state, grad, *parts),
        [EXT, EXT, PLANES, SIDE],
        {8: 0, 9: 1},
    )
    mid_2 = from_behind(side_2, "col", 1)
    grad, side_1, corner, low = call(
        late_kernel, scalars, (tab, probe, prop, mid, grad), [EXT, SIDE, CORE, EDGE], {8: 0}
    )
    mid_1 = from_behind(side_1, "col", 1)
    corner = from_behind(corner, "row", 1)
    low = from_behind(low, "row", 1)
    main, end_r = call(final_settle_kernel, (), (state, grad, corner), [(4, ROWS, COLS), CORE])
    end = from_behind(end_r, "col", 1)
    return call(last_kernel, (), (main, mid_1, mid_2, end, low), [(2, 2, ROWS, COLS)])[0]


def solution(mesh):
    in_specs = (
        P(None, None, "row", "col"),
        P(),
        P(),
        P("row", "col", None, None, None),
        P("row", "col"),
        P("row", "col", None),
        P("row", "col", None),
        P("row", "col", None),
    )
    out_specs = P(None, None, "row", "col")
    return jax.shard_map(body, mesh=mesh, in_specs=in_specs, out_specs=out_specs, check_vma=False)
```
